32 devices in a mesh: groups: 2 (over x), ctx: 16 (over z, y, core).
Axes of the slice: x: 2, y: 2, z: 4, core: 2. Of those that a mesh axis runs over, the one named last changes fastest.
Arguments:
- query: bfloat16 [8192, 6144], P(('groups', 'ctx')), parts along dimension 0, may hold values from -6 to 6
- key_rows: bfloat16 [8192, 6144], P(('groups', 'ctx')), parts along dimension 0, may hold values from -0.59765625 to 0.59765625
- value_rows: bfloat16 [8192, 6144], P(('groups', 'ctx')), parts along dimension 0, may hold values from -60 to 60
- log_decay: float32 [8192, 48], P(('groups', 'ctx')), parts along dimension 0, may hold values from -1.2 to 0
- gate_input: bfloat16 [8192, 6144], P(('groups', 'ctx')), parts along dimension 0, may hold values from -6 to 6
- residual: bfloat16 [8192, 6144], P(('groups', 'ctx')), parts along dimension 0, may hold values from -60 to 60
- attn_gain: float32 [6144], replicated, may hold values from 0.1 to 1.9
- moe_gain: float32 [6144], replicated, may hold values from 0.1 to 1.9
- expert_ids: int32 [8192, 2], P(('groups', 'ctx')), parts along dimension 0, may hold values from 0 to 15, all different within a row; in each aligned block of 256 rows (0 to 255, 256 to 511, ...) at most 40 rows name the same one
Outputs:
- expert_rows: bfloat16 [32, 640, 6144], P(('groups', 'ctx')), parts along dimension 0
The draws below stay inside these ranges and needn't reach their ends.
There are 2 independent parts, one for each index of `groups`. The reference program is written for one: setup_inputs(seed, part) draws one part's arguments, and reference() takes and returns one part's arrays. A program takes and returns all parts, laid end to end along the dimension named above; an argument that names none is the same for every part. Nothing has to cross between parts.
Inputs may be any that keep to these rules, and one draw needn't show every extreme that they name: `expert_ids`: in the rows of one device (aligned blocks of 256 rows) no expert is named more than 40 times, a bound that some block reaches; the two experts of a row differ.
All inputs are finite; a program needn't handle non-finite values.
Results may differ from the reference program's by a relative error of at most 0.0027.
Values may be sent and summed in bfloat16 or wider, within the bound.
A program may use at most 256 MiB of HBM per device.

```python
import math
import jax
import jax.numpy as jnp
import numpy as np
from jax import lax

D = 6144
HEAD_DIM = 128
HEAD_GROUP = 48
TOPK = 2
TOK_DEV = 256
PROMPT_TOKENS = 4096
EXPERTS = 16
CAP = 40
N_CTX = 16


def scaled_field(key):
    partition_count = jax.random.split(key, 3)
    column_scale = jnp.exp(jax.random.uniform(partition_count[0], (1, D), jnp.float32, jnp.log(0.3), jnp.log(3.0)))
    row_scale = jnp.exp(jax.random.uniform(partition_count[1], (PROMPT_TOKENS, 1), jnp.float32, jnp.log(0.3), jnp.log(3.0)))
    base = jnp.clip(jax.random.normal(partition_count[2], (PROMPT_TOKENS, D), jnp.float32), -6.0, 6.0)
    return (base * column_scale * row_scale).astype(jnp.bfloat16)


def draw_value_rows(key, part):
    return scaled_field(jax.random.fold_in(key, 11))


def draw_residual(key, part):
    return scaled_field(jax.random.fold_in(key, 23))


def draw_log_decay(key, part):
    partition_count = jax.random.split(jax.random.fold_in(key, 5), 7)
    share = 0.5
    fast_head = jax.random.uniform(partition_count[0], (HEAD_GROUP,), jnp.float32) < share
    slow_rate = jnp.exp(jax.random.uniform(partition_count[1], (HEAD_GROUP,), jnp.float32, jnp.log(0.05), jnp.log(0.25))) / PROMPT_TOKENS
    fast_rate = jnp.exp(jax.random.uniform(partition_count[2], (HEAD_GROUP,), jnp.float32, jnp.log(1.0 / 50.0), jnp.log(1.0 / 30.0)))
    head_decay_rate = jnp.where(fast_head, fast_rate, slow_rate)
    machine_multiplier = jnp.exp(jax.random.uniform(partition_count[3], (PROMPT_TOKENS // TOK_DEV, HEAD_GROUP), jnp.float32, jnp.log(0.5), jnp.log(2.0)))
    machine_multiplier = jnp.repeat(machine_multiplier, TOK_DEV, axis=0)
    random_noise = jax.random.uniform(partition_count[4], (PROMPT_TOKENS, HEAD_GROUP), jnp.float32, 0.5, 1.5)
    spike_positions = jax.random.randint(partition_count[5], (2,), 0, PROMPT_TOKENS)
    spike_penalty = jnp.log(jax.random.uniform(partition_count[6], (2, HEAD_GROUP), jnp.float32, 0.5, 0.8))
    spike_flags = (jnp.arange(PROMPT_TOKENS)[:, None] == spike_positions[None, :]).astype(jnp.float32)
    return -head_decay_rate[None, :] * machine_multiplier * random_noise + spike_flags @ spike_penalty


def block_levels(stream_key, shape, pieces, smallest, top_value):
    loudness = 1.0
    for dim, shards_of in pieces:
        draws = jax.random.uniform(jax.random.fold_in(jax.random.fold_in(stream_key, 6), dim), (shards_of,), jnp.float32, smallest / len(pieces), top_value / len(pieces))
        loudness = loudness * jnp.repeat(jnp.exp(draws), shape[dim] // shards_of).reshape((-1,) + (1,) * (len(shape) - 1 - dim))
    return loudness


def assign_block(own_key, own, number, rows, number_of, top, reach, skew):
    order = jax.random.permutation(own_key, number_of)
    crowded, ordinary = portions_of(number_of, rows * top, reach, skew, True), portions_of(number_of, rows * top, reach, skew, False)
    places = jnp.arange(number_of)

    def named(tallies, offset_by):
        used = int((tallies > 0).sum())
        fixed = max(1, used // 4)
        passed = fixed + (places - fixed + offset_by * (used - fixed)) % max(1, number_of - fixed)
        return jnp.zeros((number_of,), jnp.int32).at[order[jnp.where(places < fixed, places, passed)]].set(jnp.asarray(tallies, jnp.int32))

    tallies = jnp.where(number % 4 == 0, named(crowded, number // 4), named(ordinary, number - number // 4 - 1))
    mixed = jax.random.permutation(jax.random.fold_in(own, 3), number_of)
    source_of, taker = mixed[0:number_of // 2 * 2:2], mixed[1:number_of // 2 * 2:2]
    margin = jnp.minimum(tallies[source_of] - 1, reach - tallies[taker]) // 2
    margin = jnp.where((source_of == order[0]) | (taker == order[0]) | (tallies[taker] == 0), 0, jnp.maximum(margin, 0))
    passed = jax.random.randint(jax.random.fold_in(own, 4), (number_of // 2,), 0, 1 << 20) % (margin + 1)
    tallies = tallies.at[source_of].add(-passed).at[taker].add(passed)
    items = jnp.searchsorted(jnp.cumsum(tallies), jnp.arange(rows * top), side="right").astype(jnp.int32)
    table = items.reshape(top, rows).T
    table = table[jax.random.permutation(jax.random.fold_in(own, 1), rows)]
    offset_by = jax.random.randint(jax.random.fold_in(own, 2), (rows, 1), 0, top)
    return jnp.take_along_axis(table, (jnp.arange(top)[None, :] + offset_by) % top, axis=1)


def portions_of(number_of, total, bound, slope, full):
    loads = [(1 << 20) // math.isqrt(rank ** slope) + 1 for rank in range(1, number_of + 1)]
    largest = bound if full else min(bound, max(-(-total // number_of), total * loads[0] // sum(loads)))
    least = 1 if total - largest >= number_of - 1 else 0
    holding, rest = [largest] + [least] * (number_of - 1), total - largest - least * (number_of - 1)
    while rest > 0:
        free = [i for i in range(1, number_of) if holding[i] < largest] or [i for i in range(1, number_of) if holding[i] < bound]
        mass, left = sum([loads[i] for i in free]), rest
        for i in free:
            more = min(bound - holding[i], max(1, left * loads[i] // mass), rest)
            holding[i] = holding[i] + more
            rest = rest - more
    return np.array(holding)


def centred(rng, shape, scale, reach, pieces=(), kind=jnp.bfloat16):
    values = jax.random.normal(rng, shape, jnp.float32) * scale
    if len(pieces) > 0:
        values = block_levels(rng, shape, pieces, -0.22, 0.18) * values
    return jnp.clip(values, min=-reach, max=reach).astype(kind)


def setup_inputs(seed: int = 0, part: int = 0) -> dict:
    streams_of = jax.random.split(jax.random.key(seed), 10)
    part_keys = jax.random.split(jax.random.fold_in(streams_of[9], part), 10)
    query = centred(part_keys[0], (PROMPT_TOKENS, D), 1.0, 6.0, ((0, 16),))
    key_rows = centred(part_keys[1], (PROMPT_TOKENS, D), 0.1, 0.59765625, ((0, 16),))
    value_rows = draw_value_rows(jax.random.fold_in(jax.random.fold_in(streams_of[9], part), 71), part)
    log_decay = draw_log_decay(jax.random.fold_in(jax.random.fold_in(streams_of[9], part), 71), part)
    gate_input = centred(part_keys[4], (PROMPT_TOKENS, D), 1.0, 6.0, ((0, 16),))
    residual = draw_residual(jax.random.fold_in(jax.random.fold_in(streams_of[9], part), 71), part)
    attn_gain = jnp.clip(1.0 + 0.18 * jax.random.normal(streams_of[6], (D,), jnp.float32), 0.1, 1.9)
    moe_gain = jnp.clip(1.0 + 0.18 * jax.random.normal(streams_of[7], (D,), jnp.float32), 0.1, 1.9)
    expert_ids_keys = jax.random.split(jax.random.fold_in(part_keys[8], 1), PROMPT_TOKENS // TOK_DEV)
    expert_ids_turns = jax.random.permutation(jax.random.fold_in(part_keys[8], 3), PROMPT_TOKENS // TOK_DEV)
    expert_ids = jax.vmap(lambda own, number: assign_block(jax.random.fold_in(part_keys[8], 2), own, number, TOK_DEV, EXPERTS, TOPK, CAP, 2))(expert_ids_keys, expert_ids_turns).reshape((PROMPT_TOKENS, TOPK))
    return {"query": query, "key_rows": key_rows, "value_rows": value_rows, "log_decay": log_decay, "gate_input": gate_input, "residual": residual, "attn_gain": attn_gain, "moe_gain": moe_gain, "expert_ids": expert_ids}


def reference(query, key_rows, value_rows, log_decay, gate_input, residual, attn_gain, moe_gain, expert_ids):
    query_heads = query.reshape(N_CTX, TOK_DEV, HEAD_GROUP, HEAD_DIM)
    key_heads = key_rows.reshape(N_CTX, TOK_DEV, HEAD_GROUP, HEAD_DIM)
    value_heads = value_rows.reshape(N_CTX, TOK_DEV, HEAD_GROUP, HEAD_DIM)
    cumulative = jnp.cumsum(log_decay.reshape(N_CTX, TOK_DEV, HEAD_GROUP), axis=1)

    def block_summary(inputs):
        key_block, value_block, cum_block = inputs
        final_log = cum_block[-1]
        weighted_keys = (jnp.exp(final_log - cum_block)[:, :, None] * key_block.astype(jnp.float32)).astype(jnp.bfloat16)
        block_state = jnp.einsum('thd,the->hde', weighted_keys.astype(jnp.float32), value_block.astype(jnp.float32))
        return (block_state, jnp.exp(final_log))
    states, decays = lax.map(block_summary, (key_heads, value_heads, cumulative))

    def carry_step(previous, inputs):
        block_state, block_decay = inputs
        return (block_decay[:, None, None] * previous + block_state, previous)
    _, carried = lax.scan(carry_step, jnp.zeros((HEAD_GROUP, HEAD_DIM, HEAD_DIM), jnp.float32), (states, decays))
    positions = jnp.arange(TOK_DEV, dtype=jnp.int32)
    causal_mask = positions[:, None] >= positions[None, :]

    def block_output(inputs):
        query_block, key_block, value_block, cum_block, previous = inputs
        score_block = jnp.einsum('thd,shd->hts', query_block.astype(jnp.float32), key_block.astype(jnp.float32))
        cum_heads = cum_block.T
        log_gap = cum_heads[:, :, None] - cum_heads[:, None, :]
        log_gap = jnp.where(causal_mask[None], log_gap, 0.0)
        intra_weights = jnp.where(causal_mask[None], score_block * jnp.exp(log_gap), 0.0).astype(jnp.bfloat16)
        intra_out = jnp.einsum('hts,shd->thd', intra_weights.astype(jnp.float32), value_block.astype(jnp.float32))
        inter_out = jnp.exp(cum_block)[:, :, None] * jnp.einsum('thd,hde->the', query_block.astype(jnp.float32), previous, precision=lax.Precision.HIGHEST)
        return (intra_out + inter_out).reshape(TOK_DEV, D)
    attention = lax.map(block_output, (query_heads, key_heads, value_heads, cumulative, carried)).reshape(PROMPT_TOKENS, D)
    branch_out = attention * lax.rsqrt(lax.optimization_barrier(jnp.mean(attention * attention, axis=-1, keepdims=True)) + 1e-06) * attn_gain * jax.nn.sigmoid(gate_input.astype(jnp.float32))
    hidden_rows = residual.astype(jnp.float32) + branch_out
    normed_rows = (hidden_rows * lax.rsqrt(lax.optimization_barrier(jnp.mean(hidden_rows * hidden_rows, axis=-1, keepdims=True)) + 1e-06) * moe_gain).astype(jnp.bfloat16)
    pair_ids = expert_ids.reshape(N_CTX, TOK_DEV * TOPK)
    one_hot = (pair_ids[:, :, None] == jnp.arange(EXPERTS, dtype=jnp.int32)[None, None, :]).astype(jnp.int32)
    earlier_count = jnp.cumsum(one_hot, axis=1) - one_hot
    slot_index = lax.optimization_barrier(jnp.sum(earlier_count * one_hot, axis=2))
    source_block = jnp.arange(N_CTX, dtype=jnp.int32)[:, None]
    target_row = (pair_ids * (N_CTX * CAP) + source_block * CAP + slot_index).astype(jnp.int32)
    pair_rows = jnp.repeat(normed_rows, TOPK, axis=0)
    gathered = jnp.zeros((EXPERTS * N_CTX * CAP, D), jnp.bfloat16).at[target_row.reshape(-1)].set(pair_rows)
    return gathered.reshape(EXPERTS, N_CTX * CAP, D)
```

```python
import functools

import jax
import jax.numpy as jnp
from jax import lax
from jax.experimental import pallas as pl
from jax.experimental.pallas import tpu as pltpu
from jax.sharding import PartitionSpec as P

PLANE = 4
LAG = 2
PARTS = 16
F32 = jnp.float32
BF16 = jnp.bfloat16


def dot(a, b, dims=((1,), (0,)), precision=None):
    return lax.dot_general(a, b, (dims, ((), ())), preferred_element_type=F32, precision=precision)


def attend_kernel(
    sizes, q_hbm, k_hbm, v_hbm, ld_ref, gate_hbm, res_hbm, again_ref, mgain_ref, ids_ref, out_ref,
    q, k, v, gate, res, att, cum, tail_w, head_w, cum_t, ss, disp, st, dec, rst, rdec, cin, cout, cs, cr,
    goal, goal_in, gated, landed, near, relay,
    in_sem, a_send, a_recv, d_send, d_recv, b_send, b_recv, c_send, c_recv,
    g_send, g_recv, l_send, l_recv, n_send, n_recv, r_send, r_recv,
):
    n, heads, hd, cap, capp = sizes
    normed = k
    T, D = att.shape
    hq = heads // PLANE
    planes = n // PLANE
    me = lax.axis_index("ctx")
    plane, rank = me // PLANE, me % PLANE
    half_n = n // 2
    half_p = planes // 2
    upper = (plane >= half_p).astype(jnp.int32)
    base = upper * half_n
    local = me - base
    inner = jnp.where(upper == 1, plane - half_p, half_p - 1 - plane)
    outer = jnp.where(upper == 1, plane - half_p, plane)
    lander = jnp.where(upper == 1, half_p - 1 - outer // 2, half_p + outer // 2) * PLANE + rank
    land_slot = outer % 2
    lands = inner < half_p // 2
    far = jnp.minimum(2 * inner, half_p - 2) + (1 - upper) * half_p

    def peer(d):
        return plane * PLANE + (rank + d) % PLANE

    loads = [
        pltpu.make_async_copy(s, t, in_sem.at[i])
        for i, (s, t) in enumerate(((k_hbm, k), (v_hbm, v), (q_hbm, q), (gate_hbm, gate), (res_hbm, res)))
    ]
    for load in loads:
        load.start()

    barrier = pltpu.get_barrier_semaphore()
    for d in range(1, n):
        pl.semaphore_signal(
            barrier, inc=1, device_id={"ctx": (me + d) % n}, device_id_type=pl.DeviceIdType.MESH)

    ti = lax.broadcasted_iota(jnp.int32, (T, T), 0)
    si = lax.broadcasted_iota(jnp.int32, (T, T), 1)
    ld = ld_ref[...]
    cum[...] = dot((ti >= si).astype(F32), ld, ((1,), (1,)), precision=lax.Precision.HIGHEST)
    tail_w[...] = jnp.exp(cum[T - 1 : T, :] - cum[...])
    head_w[...] = jnp.exp(cum[...])
    cum_t[...] = dot(ld, (ti <= si).astype(F32), precision=lax.Precision.HIGHEST)
    lane_head = lax.broadcasted_iota(jnp.int32, (T, heads), 1)

    def cols(h):
        return pl.ds(pl.multiple_of(h * hd, hd), hd)

    def column(ref, h):
        return jnp.sum(jnp.where(lane_head == h, ref[...], 0.0), axis=1, keepdims=True)

    @pl.when(plane == 0)
    def _():
        cin[...] = jnp.zeros_like(cin)

    pl.semaphore_wait(barrier, n - 1)

    loads[0].wait()
    loads[1].wait()

    def a_copies(d):
        to = {"ctx": peer(d)}
        return (
            pltpu.make_async_remote_copy(
                st.at[d - 1], rst.at[d], a_send.at[d], a_recv.at[d],
                device_id=to, device_id_type=pl.DeviceIdType.MESH),
            pltpu.make_async_remote_copy(
                dec.at[d - 1], rdec.at[d], d_send.at[d], d_recv.at[d],
                device_id=to, device_id_type=pl.DeviceIdType.MESH),
        )

    for d in (2, 1, 3, 0):
        quarter = (rank + d) % PLANE
        s_to, d_to = (rst.at[0], rdec.at[0]) if d == 0 else (st.at[d - 1], dec.at[d - 1])

        def state_step(i, _, quarter=quarter, s_to=s_to, d_to=d_to):
            h = quarter * hq + i
            last = cum_t[pl.ds(h, 1), :][:, T - 1 : T]
            wk = (column(tail_w, h) * k[:, cols(h)].astype(F32)).astype(BF16)
            s_to[i] = dot(wk, v[:, cols(h)], ((0,), (0,))).astype(BF16)
            d_to[pl.ds(i, 1), :] = jnp.broadcast_to(jnp.exp(last), (1, 128))
            return 0

        lax.fori_loop(0, hq, state_step, 0, unroll=2)
        if d:
            for c in a_copies(d):
                c.start()

    loads[2].wait()
    half = T // 2
    mask_lo = lax.broadcasted_iota(jnp.int32, (half, half), 0) >= lax.broadcasted_iota(jnp.int32, (half, half), 1)
    mask_hi = lax.broadcasted_iota(jnp.int32, (half, T), 0) + half >= lax.broadcasted_iota(jnp.int32, (half, T), 1)

    def intra_step(h, _):
        col = column(cum, h)
        row = cum_t[pl.ds(h, 1), :]
        qh, kh, vh = q[:, cols(h)], k[:, cols(h)], v[:, cols(h)]
        s_lo = dot(qh[:half], kh[:half], ((1,), (1,)))
        w_lo = jnp.where(mask_lo, s_lo * jnp.exp(col[:half] - row[:, :half]), 0.0).astype(BF16)
        att[:half, cols(h)] = dot(w_lo, vh[:half])
        s_hi = dot(qh[half:], kh, ((1,), (1,)))
        w_hi = jnp.where(mask_hi, s_hi * jnp.exp(col[half:] - row), 0.0).astype(BF16)
        att[half:, cols(h)] = dot(w_hi, vh)
        return 0

    lax.fori_loop(0, heads, intra_step, 0, unroll=2)

    loads[3].wait()

    def gate_step(h, _):
        gated[:, cols(h)] = jax.nn.sigmoid(gate[:, cols(h)].astype(F32)) * again_ref[:, cols(h)]
        return 0

    gates = jnp.where(plane == 0, 0, heads // 2)

    def gate_pair(i, z):
        return gate_step(2 * i + 1, gate_step(2 * i, z))

    lax.fori_loop(0, gates, gate_pair, 0)

    for d in range(1, PLANE):
        for c in a_copies(d):
            c.wait_recv()

    def b_copy(c):
        part = pl.ds(c, 1)
        return pltpu.make_async_remote_copy(
            cout.at[part], cin.at[part], b_send.at[c], b_recv.at[c],
            device_id={"ctx": jnp.minimum(me + PLANE, n - 1)}, device_id_type=pl.DeviceIdType.MESH)

    def c_copy(d, c):
        part = pl.ds(c, 1)
        return pltpu.make_async_remote_copy(
            cs.at[d, part], cr.at[d, part], c_send.at[d, c], c_recv.at[d, c],
            device_id={"ctx": peer(d)}, device_id_type=pl.DeviceIdType.MESH)

    def inter_step(i):
        for d in range(PLANE):
            if d:
                c_copy(d, i).wait_recv()
            h = (rank - d + PLANE) % PLANE * hq + i
            carried = cs[d, i] if d == 0 else cr[d, i]
            x = att[:, cols(h)] + column(head_w, h) * dot(q[:, cols(h)], carried)
            att[:, cols(h)] = x
            ss[...] += x * x

    ss[...] = jnp.zeros_like(ss)

    def scan_step(c, _):
        @pl.when(plane > 0)
        def _():
            b_copy(c).wait_recv()

        x = cin[c]
        for i in range(PLANE):
            src = (rank - i + PLANE) % PLANE
            to = (i - rank + PLANE) % PLANE
            cs[to, c] = x.astype(BF16)
            x = rdec[src, pl.ds(c, 1), :] * x + rst[src, c].astype(F32)
        cout[c] = x

        @pl.when(plane < planes - 1)
        def _():
            b_copy(c).start()

        for d in (2, 1, 3):
            c_copy(d, c).start()

        @pl.when(c >= LAG)
        def _():
            inter_step(c - LAG)

        return 0

    lax.fori_loop(0, hq, scan_step, 0)

    lax.fori_loop(gates, heads // 2, gate_pair, 0)

    experts = n
    ids = ids_ref[...]
    ex = lax.broadcasted_iota(jnp.int32, (experts, T), 0)
    first, second = (ids[0:1, :] == ex).astype(F32), (ids[1:2, :] == ex).astype(F32)
    earlier = dot((first + second).astype(BF16), (ti < si).astype(BF16))
    place = earlier + (ex * capp).astype(F32)
    row_of = [jnp.sum(one * place, axis=0, keepdims=True) for one in (first, second)]
    goal[0:1, :] = row_of[0]
    goal[1:2, :] = row_of[1]
    goal[2:8, :] = jnp.full((6, T), -1.0, F32)
    goal_copy = pltpu.make_async_remote_copy(
        goal, goal_in.at[land_slot], g_send, g_recv.at[land_slot],
        device_id={"ctx": lander}, device_id_type=pl.DeviceIdType.MESH)
    goal_copy.start()
    slot = lax.broadcasted_iota(jnp.int32, (half_n * capp, T), 0) + base * capp
    slot = slot.astype(F32)
    disp[0] = ((slot == row_of[0]) | (slot == row_of[1])).astype(BF16)

    for i in range(hq - LAG, hq):
        inter_step(i)

    rstd = lax.rsqrt(jnp.sum(ss[...], axis=1, keepdims=True) / D + 1e-6)
    loads[4].wait()
    ss[...] = jnp.zeros_like(ss)

    def branch_step(h, _):
        x = att[:, cols(h)] * rstd * gated[:, cols(h)]
        x = res[:, cols(h)].astype(F32) + x
        att[:, cols(h)] = x
        ss[...] += x * x
        return 0

    lax.fori_loop(0, heads, branch_step, 0, unroll=2)
    rstd2 = lax.rsqrt(jnp.sum(ss[...], axis=1, keepdims=True) / D + 1e-6)
    wide = D // PARTS

    def part(c):
        return pl.ds(pl.multiple_of(c * wide, wide), wide)

    def l_copy(c):
        return pltpu.make_async_remote_copy(
            normed.at[:, part(c)], landed.at[land_slot, :, part(c)], l_send.at[c], l_recv.at[land_slot, c],
            device_id={"ctx": lander}, device_id_type=pl.DeviceIdType.MESH)

    def norm_step(c, _):
        normed[:, part(c)] = (att[:, part(c)] * rstd2 * mgain_ref[:, part(c)]).astype(BF16)
        l_copy(c).start()
        return 0

    lax.fori_loop(0, PARTS, norm_step, 0)

    def near_step(c, _):
        rows = dot(disp[0], normed[:, part(c)]).astype(BF16)
        for e in range(half_n):
            near[e, :, part(c)] = rows[e * capp : e * capp + cap]
        return 0

    lax.fori_loop(0, PARTS, near_step, 0)

    def n_copy(j):
        e = (local + j) % half_n
        return pltpu.make_async_remote_copy(
            near.at[e], out_ref.at[me], n_send.at[j], n_recv.at[j],
            device_id={"ctx": base + e}, device_id_type=pl.DeviceIdType.MESH)

    own = pltpu.make_async_copy(near.at[local], out_ref.at[me], n_send.at[0])
    own.start()
    for j in range(1, half_n):
        n_copy(j).start()

    @pl.when(lands)
    def _():
        for x in range(2):
            pltpu.make_async_remote_copy(
                goal, goal_in.at[x], g_send, g_recv.at[x],
                device_id={"ctx": lander}, device_id_type=pl.DeviceIdType.MESH).wait_recv()
            disp[1 + x] = ((slot == goal_in[x, 0:1, :]) | (slot == goal_in[x, 1:2, :])).astype(BF16)

        def relay_step(s, _):
            x = jnp.where(s < PARTS, 1 - upper, upper)
            c = s % PARTS
            block = (far + x) * PLANE + rank
            at = block - (half_n - base)
            pltpu.make_async_remote_copy(
                normed.at[:, part(c)], landed.at[x, :, part(c)], l_send.at[c], l_recv.at[x, c],
                device_id={"ctx": lander}, device_id_type=pl.DeviceIdType.MESH).wait_recv()
            rows = dot(disp[1 + x], landed[x, :, part(c)]).astype(BF16)
            for e in range(half_n):
                relay[x, e, :, part(c)] = rows[e * capp : e * capp + cap]
            for j in range(1, half_n):
                e = (local + j) % half_n
                pltpu.make_async_remote_copy(
                    relay.at[x, e, :, part(c)], out_ref.at[block, :, part(c)],
                    r_send.at[x, j], r_recv.at[at],
                    device_id={"ctx": base + e}, device_id_type=pl.DeviceIdType.MESH).start()
            pltpu.make_async_copy(
                relay.at[x, local, :, part(c)], out_ref.at[block, :, part(c)], r_recv.at[at]).start()
            return 0

        lax.fori_loop(0, 2 * PARTS, relay_step, 0)
        for x in range(2):
            for j in range(1, half_n):
                pltpu.make_async_remote_copy(
                    relay.at[x, 0], out_ref.at[me], r_send.at[x, j], r_recv.at[0],
                    device_id={"ctx": lander}, device_id_type=pl.DeviceIdType.MESH).wait_send()

    own.wait()
    for j in range(1, half_n):
        n_copy(j).wait()
    for b in range(half_n):
        pltpu.make_async_copy(near.at[0], out_ref.at[half_n - base + b], r_recv.at[b]).wait()
    lax.fori_loop(0, PARTS, lambda c, z: (l_copy(c).wait_send(), z)[1], 0)
    goal_copy.wait_send()
    for d in range(1, PLANE):
        for c in a_copies(d):
            c.wait_send()
        lax.fori_loop(0, hq, lambda c, z, d=d: (c_copy(d, c).wait_send(), z)[1], 0)

    @pl.when(plane < planes - 1)
    def _():
        lax.fori_loop(0, hq, lambda c, z: (b_copy(c).wait_send(), z)[1], 0)


def body(query, key_rows, value_rows, log_decay, gate_input, residual, attn_gain, moe_gain, expert_ids):
    T, D = query.shape
    heads = log_decay.shape[1]
    hd = D // heads
    n = lax.axis_size("ctx")
    experts = n
    cap = 5 * T * expert_ids.shape[1] // (4 * experts)
    hq = heads // PLANE
    hp = -(-hq // 8) * 8
    capp = -(-cap // 16) * 16
    half_n = n // 2
    vm, anyspace = pl.BlockSpec(memory_space=pltpu.VMEM), pl.BlockSpec(memory_space=pl.ANY)
    V, DMA = pltpu.VMEM, pltpu.SemaphoreType.DMA
    arrived = pl.pallas_call(
        functools.partial(attend_kernel, (n, heads, hd, cap, capp)),
        out_shape=jax.ShapeDtypeStruct((n, cap, D), BF16),
        in_specs=[anyspace] * 3 + [vm] + [anyspace] * 2 + [vm] * 3,
        out_specs=anyspace,
        scratch_shapes=[
            V((T, D), BF16), V((T, D), BF16), V((T, D), BF16), V((T, D), BF16), V((T, D), BF16),
            V((T, D), F32), V((T, heads), F32), V((T, heads), F32), V((T, heads), F32), V((heads, T), F32), V((T, hd), F32),
            V((3, half_n * capp, T), BF16),
            V((PLANE - 1, hq, hd, hd), BF16), V((PLANE - 1, hp, 128), F32),
            V((PLANE, hq, hd, hd), BF16), V((PLANE, hp, 128), F32),
            V((hq, hd, hd), F32), V((hq, hd, hd), F32),
            V((PLANE, hq, hd, hd), BF16), V((PLANE, hq, hd, hd), BF16),
            V((8, T), F32), V((2, 8, T), F32), V((T, D), F32), V((2, T, D), BF16),
            V((half_n, cap, D), BF16), V((2, half_n, cap, D), BF16),
            DMA((5,)), DMA((PLANE,)), DMA((PLANE,)), DMA((PLANE,)), DMA((PLANE,)),
            DMA((hq,)), DMA((hq,)), DMA((PLANE, hq)), DMA((PLANE, hq)),
            DMA, DMA((2,)), DMA((PARTS,)), DMA((2, PARTS)), DMA((half_n,)), DMA((half_n,)),
            DMA((2, half_n)), DMA((half_n,)),
        ],
        compiler_params=pltpu.CompilerParams(
            collective_id=0, has_side_effects=True, vmem_limit_bytes=67043328
        ),
        name="attend",
    )(
        query, key_rows, value_rows, log_decay.T, gate_input, residual,
        attn_gain.reshape(1, D), moe_gain.reshape(1, D), expert_ids.T,
    )
    return arrived.reshape(1, n * cap, D)


def solution(mesh):
    rows = P(("groups", "ctx"), None)
    return jax.shard_map(
        body, mesh=mesh, in_specs=(rows,) * 6 + (P(), P(), rows),
        out_specs=P(("groups", "ctx"), None, None), check_vma=False,
    )
```

```python
import functools

import jax
import jax.numpy as jnp
from jax import lax
from jax.experimental import pallas as pl
from jax.experimental.pallas import tpu as pltpu
from jax.sharding import PartitionSpec as P

PLANE = 4
START = 1
HOP = 3
LAG = 4
PARTS = 16
F32 = jnp.float32
BF16 = jnp.bfloat16


def dot(a, b, dims=((1,), (0,)), precision=None):
    return lax.dot_general(a, b, (dims, ((), ())), preferred_element_type=F32, precision=precision)


def attend_kernel(
    sizes, q_hbm, k_hbm, v_hbm, ld_ref, gate_hbm, res_hbm, again_ref, mgain_ref, ids_ref, out_ref,
    q, k, v, gate, res, att, cum, tail_w, head_w, cum_t, ss, disp,
    dec, pdec, cdec, odec, own, st, rst, sx, rx, cin, cout, xs, xr, co, cs, cr,
    goal, goal_in, gated, landed, near, relay,
    in_sem, d_send, d_recv, e_send, e_recv, a_send, a_recv, x_send, x_recv, b_send, b_recv,
    y_send, y_recv, c_send, c_recv,
    g_send, g_recv, l_send, l_recv, n_send, n_recv, r_send, r_recv,
):
    n, heads, hd, cap, capp = sizes
    normed = k
    T, D = att.shape
    hq = heads // PLANE
    planes = n // PLANE
    me = lax.axis_index("ctx")
    plane, rank = me // PLANE, me % PLANE
    half_n = n // 2
    half_p = planes // 2
    upper = (plane >= half_p).astype(jnp.int32)
    base = upper * half_n
    local = me - base
    inner = jnp.where(upper == 1, plane - half_p, half_p - 1 - plane)
    outer = jnp.where(upper == 1, plane - half_p, plane)
    lander = jnp.where(upper == 1, half_p - 1 - outer // 2, half_p + outer // 2) * PLANE + rank
    land_slot = outer % 2
    lands = inner < half_p // 2
    far = jnp.minimum(2 * inner, half_p - 2) + (1 - upper) * half_p

    core, chip = rank % 2, rank // 2
    first_core, first_chip = core == 0, chip == 0
    partner = me + 1 - 2 * core
    across = me + 2 - 4 * chip

    def remote(src, dst, send, recv, to):
        return pltpu.make_async_remote_copy(
            src, dst, send, recv, device_id={"ctx": to}, device_id_type=pl.DeviceIdType.MESH)

    def head_of(far_chip, far_core, i):
        c = 1 - chip if far_chip else chip
        return (2 * c + (1 - core if far_core else core)) * hq + i

    loads = [
        pltpu.make_async_copy(s, t, in_sem.at[i])
        for i, (s, t) in enumerate(((k_hbm, k), (v_hbm, v), (q_hbm, q), (gate_hbm, gate), (res_hbm, res)))
    ]
    for load in loads:
        load.start()

    barrier = pltpu.get_barrier_semaphore()
    for d in range(1, n):
        pl.semaphore_signal(
            barrier, inc=1, device_id={"ctx": (me + d) % n}, device_id_type=pl.DeviceIdType.MESH)

    ti = lax.broadcasted_iota(jnp.int32, (T, T), 0)
    si = lax.broadcasted_iota(jnp.int32, (T, T), 1)
    ld = ld_ref[...]
    cum[...] = dot((ti >= si).astype(F32), ld, ((1,), (1,)), precision=lax.Precision.HIGHEST)
    tail_w[...] = jnp.exp(cum[T - 1 : T, :] - cum[...])
    head_w[...] = jnp.exp(cum[...])
    cum_t[...] = dot(ld, (ti <= si).astype(F32), precision=lax.Precision.HIGHEST)
    lane_head = lax.broadcasted_iota(jnp.int32, (T, heads), 1)

    def cols(h):
        return pl.ds(pl.multiple_of(h * hd, hd), hd)

    def column(ref, h):
        return jnp.sum(jnp.where(lane_head == h, ref[...], 0.0), axis=1, keepdims=True)

    dec[...] = jnp.broadcast_to(jnp.exp(cum_t[:, T - 1 : T]), dec.shape)

    @pl.when(plane == 0)
    def _():
        cin[...] = jnp.zeros_like(cin)

    loads[0].wait()
    loads[1].wait()

    def state(h):
        wk = (column(tail_w, h) * k[:, cols(h)].astype(F32)).astype(BF16)
        return dot(wk, v[:, cols(h)], ((0,), (0,)))

    d_copy = remote(dec, pdec, d_send, d_recv, partner)
    e_copy = remote(cdec, odec, e_send, e_recv, across)

    def a_copy(a):
        return remote(st.at[a], rst.at[a], a_send.at[a], a_recv.at[a], partner)

    def x_copy(i):
        return remote(sx.at[i], rx.at[i], x_send.at[i], x_recv.at[i], across)

    def b_copy(i):
        return remote(cout.at[i], cin.at[i], b_send.at[i], b_recv.at[i], jnp.minimum(me + PLANE, n - 1))

    def y_copy(i):
        return remote(xs.at[i], xr.at[i], y_send.at[i], y_recv.at[i], across)

    def c_copy(a, i):
        return remote(cs.at[a, i], cr.at[a, i], c_send.at[a, i], c_recv.at[a, i], partner)

    def row(ref, h):
        return ref[pl.ds(h, 1), :]

    def send_state(a):
        def step(i, z):
            st[a, i] = state(head_of(a, 1, i))
            return z
        return step

    def keep_state(a):
        def step(i, z):
            own[a, i] = state(head_of(a, 0, i))
            return z
        return step

    def both(a, i):
        h = head_of(a, 0, i)
        mine, theirs = own[a, i], rst[a, i]
        early, late = jnp.where(first_core, mine, theirs), jnp.where(first_core, theirs, mine)
        return jnp.where(first_core, row(pdec, h), row(dec, h)) * early + late

    lax.fori_loop(0, hq, send_state(1), 0, unroll=2)
    pl.semaphore_wait(barrier, n - 1)
    a_copy(1).start()
    d_copy.start()
    lax.fori_loop(0, hq, keep_state(1), 0, unroll=2)
    d_copy.wait_recv()
    cdec[...] = dec[...] * pdec[...]
    e_copy.start()
    a_copy(1).wait_recv()

    def across_step(i, z):
        sx[i] = both(1, i).astype(BF16)
        x_copy(i).start()
        return send_state(0)(i, z)

    lax.fori_loop(0, hq, across_step, 0)
    a_copy(0).start()
    lax.fori_loop(0, hq, keep_state(0), 0, unroll=2)
    a_copy(0).wait_recv()
    e_copy.wait_recv()

    def give(a, i, x):
        h = head_of(a, 0, i)
        after = (jnp.where(first_core, row(dec, h), row(pdec, h)) * x
                 + jnp.where(first_core, own[a, i], rst[a, i])).astype(BF16)
        x = x.astype(BF16)
        co[a, i] = jnp.where(first_core, x, after)
        cs[a, i] = jnp.where(first_core, after, x)
        c_copy(a, i).start()

    def scan_step(i):
        @pl.when(plane > 0)
        def _():
            b_copy(i).wait_recv()

        x_copy(i).wait_recv()
        h = head_of(0, 0, i)
        mine, theirs = both(0, i), rx[i].astype(F32)
        d_mine, d_theirs = row(cdec, h), row(odec, h)
        x = cin[i].astype(F32)
        mid = jnp.where(first_chip, d_mine, d_theirs) * x + jnp.where(first_chip, mine, theirs)
        last = jnp.where(first_chip, d_theirs, d_mine) * mid + jnp.where(first_chip, theirs, mine)
        cout[i] = last.astype(BF16)

        @pl.when(plane < planes - 1)
        def _():
            b_copy(i).start()

        xs[i] = jnp.where(first_chip, mid, x).astype(BF16)
        y_copy(i).start()
        give(0, i, jnp.where(first_chip, x, mid))

    def far_step(i):
        y_copy(i).wait_recv()
        give(1, i, xr[i].astype(F32))

    loads[2].wait()
    half = T // 2
    mask_lo = lax.broadcasted_iota(jnp.int32, (half, half), 0) >= lax.broadcasted_iota(jnp.int32, (half, half), 1)
    mask_hi = lax.broadcasted_iota(jnp.int32, (half, T), 0) + half >= lax.broadcasted_iota(jnp.int32, (half, T), 1)

    def intra_step(h, _):
        col = column(cum, h)
        row = cum_t[pl.ds(h, 1), :]
        qh, kh, vh = q[:, cols(h)], k[:, cols(h)], v[:, cols(h)]
        s_lo = dot(qh[:half], kh[:half], ((1,), (1,)))
        w_lo = jnp.where(mask_lo, s_lo * jnp.exp(col[:half] - row[:, :half]), 0.0).astype(BF16)
        att[:half, cols(h)] = dot(w_lo, vh[:half])
        s_hi = dot(qh[half:], kh, ((1,), (1,)))
        w_hi = jnp.where(mask_hi, s_hi * jnp.exp(col[half:] - row), 0.0).astype(BF16)
        att[half:, cols(h)] = dot(w_hi, vh)
        return 0

    begin = START + HOP * plane

    def mixed_step(i, z):
        @pl.when(i < heads // 2)
        def _():
            intra_step(2 * i, 0)
            intra_step(2 * i + 1, 0)

        @pl.when((i >= begin) & (i < begin + hq))
        def _():
            scan_step(i - begin)

        @pl.when((i >= begin + LAG) & (i < begin + LAG + hq))
        def _():
            far_step(i - begin - LAG)

        return z

    lax.fori_loop(0, jnp.maximum(heads // 2, begin + LAG + hq), mixed_step, 0)

    loads[3].wait()

    def gate_step(h, _):
        gated[:, cols(h)] = jax.nn.sigmoid(gate[:, cols(h)].astype(F32)) * again_ref[:, cols(h)]
        return 0

    lax.fori_loop(0, heads, gate_step, 0, unroll=2)

    def inter_step(h, carried):
        x = att[:, cols(h)] + column(head_w, h) * dot(q[:, cols(h)], carried)
        att[:, cols(h)] = x
        ss[...] += x * x

    ss[...] = jnp.zeros_like(ss)

    def inter_all(i, z):
        for a in range(2):
            inter_step(head_of(a, 0, i), co[a, i])
            c_copy(a, i).wait_recv()
            inter_step(head_of(a, 1, i), cr[a, i])
        return z

    lax.fori_loop(0, hq, inter_all, 0)

    experts = n
    ids = ids_ref[...]
    ex = lax.broadcasted_iota(jnp.int32, (experts, T), 0)
    first, second = (ids[0:1, :] == ex).astype(F32), (ids[1:2, :] == ex).astype(F32)
    earlier = dot((first + second).astype(BF16), (ti < si).astype(BF16))
    place = earlier + (ex * capp).astype(F32)
    row_of = [jnp.sum(one * place, axis=0, keepdims=True) for one in (first, second)]
    goal[0:1, :] = row_of[0]
    goal[1:2, :] = row_of[1]
    goal[2:8, :] = jnp.full((6, T), -1.0, F32)
    goal_copy = pltpu.make_async_remote_copy(
        goal, goal_in.at[land_slot], g_send, g_recv.at[land_slot],
        device_id={"ctx": lander}, device_id_type=pl.DeviceIdType.MESH)
    goal_copy.start()
    slot = lax.broadcasted_iota(jnp.int32, (half_n * capp, T), 0) + base * capp
    slot = slot.astype(F32)
    disp[0] = ((slot == row_of[0]) | (slot == row_of[1])).astype(BF16)

    rstd = lax.rsqrt(jnp.sum(ss[...], axis=1, keepdims=True) / D + 1e-6)
    loads[4].wait()
    ss[...] = jnp.zeros_like(ss)

    def branch_step(h, _):
        x = att[:, cols(h)] * rstd * gated[:, cols(h)]
        x = res[:, cols(h)].astype(F32) + x
        att[:, cols(h)] = x
        ss[...] += x * x
        return 0

    lax.fori_loop(0, heads, branch_step, 0, unroll=2)
    rstd2 = lax.rsqrt(jnp.sum(ss[...], axis=1, keepdims=True) / D + 1e-6)
    wide = D // PARTS

    def part(c):
        return pl.ds(pl.multiple_of(c * wide, wide), wide)

    def l_copy(c):
        return pltpu.make_async_remote_copy(
            normed.at[:, part(c)], landed.at[land_slot, :, part(c)], l_send.at[c], l_recv.at[land_slot, c],
            device_id={"ctx": lander}, device_id_type=pl.DeviceIdType.MESH)

    def norm_step(c, _):
        normed[:, part(c)] = (att[:, part(c)] * rstd2 * mgain_ref[:, part(c)]).astype(BF16)
        l_copy(c).start()
        return 0

    lax.fori_loop(0, PARTS, norm_step, 0)

    def near_step(c, _):
        rows = dot(disp[0], normed[:, part(c)]).astype(BF16)
        for e in range(half_n):
            near[e, :, part(c)] = rows[e * capp : e * capp + cap]
        return 0

    lax.fori_loop(0, PARTS, near_step, 0)

    def n_copy(j):
        e = (local + j) % half_n
        return pltpu.make_async_remote_copy(
            near.at[e], out_ref.at[me], n_send.at[j], n_recv.at[j],
            device_id={"ctx": base + e}, device_id_type=pl.DeviceIdType.MESH)

    keep = pltpu.make_async_copy(near.at[local], out_ref.at[me], n_send.at[0])
    keep.start()
    for j in range(1, half_n):
        n_copy(j).start()

    @pl.when(lands)
    def _():
        for x in range(2):
            pltpu.make_async_remote_copy(
                goal, goal_in.at[x], g_send, g_recv.at[x],
                device_id={"ctx": lander}, device_id_type=pl.DeviceIdType.MESH).wait_recv()
            disp[1 + x] = ((slot == goal_in[x, 0:1, :]) | (slot == goal_in[x, 1:2, :])).astype(BF16)

        def relay_step(s, _):
            x = jnp.where(s < PARTS, 1 - upper, upper)
            c = s % PARTS
            block = (far + x) * PLANE + rank
            at = block - (half_n - base)
            pltpu.make_async_remote_copy(
                normed.at[:, part(c)], landed.at[x, :, part(c)], l_send.at[c], l_recv.at[x, c],
                device_id={"ctx": lander}, device_id_type=pl.DeviceIdType.MESH).wait_recv()
            rows = dot(disp[1 + x], landed[x, :, part(c)]).astype(BF16)
            for e in range(half_n):
                relay[x, e, :, part(c)] = rows[e * capp : e * capp + cap]
            for j in range(1, half_n):
                e = (local + j) % half_n
                pltpu.make_async_remote_copy(
                    relay.at[x, e, :, part(c)], out_ref.at[block, :, part(c)],
                    r_send.at[x, j], r_recv.at[at],
                    device_id={"ctx": base + e}, device_id_type=pl.DeviceIdType.MESH).start()
            pltpu.make_async_copy(
                relay.at[x, local, :, part(c)], out_ref.at[block, :, part(c)], r_recv.at[at]).start()
            return 0

        lax.fori_loop(0, 2 * PARTS, relay_step, 0)
        for x in range(2):
            for j in range(1, half_n):
                pltpu.make_async_remote_copy(
                    relay.at[x, 0], out_ref.at[me], r_send.at[x, j], r_recv.at[0],
                    device_id={"ctx": lander}, device_id_type=pl.DeviceIdType.MESH).wait_send()

    keep.wait()
    for j in range(1, half_n):
        n_copy(j).wait()
    for b in range(half_n):
        pltpu.make_async_copy(near.at[0], out_ref.at[half_n - base + b], r_recv.at[b]).wait()
    lax.fori_loop(0, PARTS, lambda c, z: (l_copy(c).wait_send(), z)[1], 0)
    goal_copy.wait_send()
    d_copy.wait_send()
    e_copy.wait_send()
    for a in range(2):
        a_copy(a).wait_send()

    def sent(i, z):
        x_copy(i).wait_send()
        y_copy(i).wait_send()
        for a in range(2):
            c_copy(a, i).wait_send()
        return z

    lax.fori_loop(0, hq, sent, 0)

    @pl.when(plane < planes - 1)
    def _():
        lax.fori_loop(0, hq, lambda i, z: (b_copy(i).wait_send(), z)[1], 0)


def body(query, key_rows, value_rows, log_decay, gate_input, residual, attn_gain, moe_gain, expert_ids):
    T, D = query.shape
    heads = log_decay.shape[1]
    hd = D // heads
    n = lax.axis_size("ctx")
    experts = n
    cap = 5 * T * expert_ids.shape[1] // (4 * experts)
    hq = heads // PLANE
    capp = -(-cap // 16) * 16
    half_n = n // 2
    vm, anyspace = pl.BlockSpec(memory_space=pltpu.VMEM), pl.BlockSpec(memory_space=pl.ANY)
    V, DMA = pltpu.VMEM, pltpu.SemaphoreType.DMA
    arrived = pl.pallas_call(
        functools.partial(attend_kernel, (n, heads, hd, cap, capp)),
        out_shape=jax.ShapeDtypeStruct((n, cap, D), BF16),
        in_specs=[anyspace] * 3 + [vm] + [anyspace] * 2 + [vm] * 3,
        out_specs=anyspace,
        scratch_shapes=[
            V((T, D), BF16), V((T, D), BF16), V((T, D), BF16), V((T, D), BF16), V((T, D), BF16),
            V((T, D), F32), V((T, heads), F32), V((T, heads), F32), V((T, heads), F32), V((heads, T), F32), V((T, hd), F32),
            V((3, half_n * capp, T), BF16),
            V((heads, 128), F32), V((heads, 128), F32), V((heads, 128), F32), V((heads, 128), F32),
            V((2, hq, hd, hd), F32), V((2, hq, hd, hd), F32), V((2, hq, hd, hd), F32),
            V((hq, hd, hd), BF16), V((hq, hd, hd), BF16), V((hq, hd, hd), BF16), V((hq, hd, hd), BF16),
            V((hq, hd, hd), BF16), V((hq, hd, hd), BF16),
            V((2, hq, hd, hd), BF16), V((2, hq, hd, hd), BF16), V((2, hq, hd, hd), BF16),
            V((8, T), F32), V((2, 8, T), F32), V((T, D), F32), V((2, T, D), BF16),
            V((half_n, cap, D), BF16), V((2, half_n, cap, D), BF16),
            DMA((5,)), DMA, DMA, DMA, DMA, DMA((2,)), DMA((2,)), DMA((hq,)), DMA((hq,)), DMA((hq,)), DMA((hq,)),
            DMA((hq,)), DMA((hq,)), DMA((2, hq)), DMA((2, hq)),
            DMA, DMA((2,)), DMA((PARTS,)), DMA((2, PARTS)), DMA((half_n,)), DMA((half_n,)),
            DMA((2, half_n)), DMA((half_n,)),
        ],
        compiler_params=pltpu.CompilerParams(
            collective_id=0, has_side_effects=True, vmem_limit_bytes=67043328
        ),
        name="attend",
    )(
        query, key_rows, value_rows, log_decay.T, gate_input, residual,
        attn_gain.reshape(1, D), moe_gain.reshape(1, D), expert_ids.T,
    )
    return arrived.reshape(1, n * cap, D)


def solution(mesh):
    rows = P(("groups", "ctx"), None)
    return jax.shard_map(
        body, mesh=mesh, in_specs=(rows,) * 6 + (P(), P(), rows),
        out_specs=P(("groups", "ctx"), None, None), check_vma=False,
    )
```

```python
import functools

import jax
import jax.numpy as jnp
from jax import lax
from jax.experimental import pallas as pl
from jax.experimental.pallas import tpu as pltpu
from jax.sharding import PartitionSpec as P

PLANE = 4
START = 0
HOP = 3
LAG = 3
FAR = 11
PARTS = 24
F32 = jnp.float32
BF16 = jnp.bfloat16


def dot(a, b, dims=((1,), (0,)), precision=None):
    return lax.dot_general(a, b, (dims, ((), ())), preferred_element_type=F32, precision=precision)


def attend_kernel(
    sizes, q_hbm, k_hbm, v_hbm, ld_ref, gate_hbm, res_hbm, again_ref, mgain_ref, ids_ref, out_ref,
    q, k, v, gate, res, att, cum, tail_w, head_w, cum_t, ss, disp,
    dec, pdec, cdec, odec, own, st, rst, sx, rx, cin, cout, xs, xr, co, cs, cr,
    goal, goal_in, gated, landed, near, relay,
    in_sem, d_send, d_recv, e_send, e_recv, a_send, a_recv, x_send, x_recv, b_send, b_recv,
    y_send, y_recv, c_send, c_recv,
    g_send, g_recv, l_send, l_recv, n_send, n_recv, r_send, r_recv,
):
    n, heads, hd, cap, capp = sizes
    normed = k
    T, D = att.shape
    hq = heads // PLANE
    planes = n // PLANE
    me = lax.axis_index("ctx")
    plane, rank = me // PLANE, me % PLANE
    half_n = n // 2
    half_p = planes // 2
    upper = (plane >= half_p).astype(jnp.int32)
    base = upper * half_n
    local = me - base
    inner = jnp.where(upper == 1, plane - half_p, half_p - 1 - plane)
    outer = jnp.where(upper == 1, plane - half_p, plane)
    lander = jnp.where(upper == 1, half_p - 1 - outer // 2, half_p + outer // 2) * PLANE + rank
    land_slot = outer % 2
    lands = inner < half_p // 2
    far = jnp.minimum(2 * inner, half_p - 2) + (1 - upper) * half_p

    core, chip = rank % 2, rank // 2
    first_core, first_chip = core == 0, chip == 0
    partner = me + 1 - 2 * core
    across = me + 2 - 4 * chip

    def remote(src, dst, send, recv, to):
        return pltpu.make_async_remote_copy(
            src, dst, send, recv, device_id={"ctx": to}, device_id_type=pl.DeviceIdType.MESH)

    def head_of(far_chip, far_core, i):
        c = 1 - chip if far_chip else chip
        return (2 * c + (1 - core if far_core else core)) * hq + i

    loads = [
        pltpu.make_async_copy(s, t, in_sem.at[i])
        for i, (s, t) in enumerate(((k_hbm, k), (v_hbm, v), (q_hbm, q), (gate_hbm, gate), (res_hbm, res)))
    ]
    for load in loads:
        load.start()

    barrier = pltpu.get_barrier_semaphore()
    for d in range(1, n):
        pl.semaphore_signal(
            barrier, inc=1, device_id={"ctx": (me + d) % n}, device_id_type=pl.DeviceIdType.MESH)

    ti = lax.broadcasted_iota(jnp.int32, (T, T), 0)
    si = lax.broadcasted_iota(jnp.int32, (T, T), 1)
    ld = ld_ref[...]
    cum[...] = dot((ti >= si).astype(F32), ld, ((1,), (1,)), precision=lax.Precision.HIGHEST)
    tail_w[...] = jnp.exp(cum[T - 1 : T, :] - cum[...])
    head_w[...] = jnp.exp(cum[...])
    cum_t[...] = dot(ld, (ti <= si).astype(F32), precision=lax.Precision.HIGHEST)
    lane_head = lax.broadcasted_iota(jnp.int32, (T, heads), 1)

    def cols(h):
        return pl.ds(pl.multiple_of(h * hd, hd), hd)

    def column(ref, h):
        return jnp.sum(jnp.where(lane_head == h, ref[...], 0.0), axis=1, keepdims=True)

    dec[...] = jnp.broadcast_to(jnp.exp(cum_t[:, T - 1 : T]), dec.shape)

    @pl.when(plane == 0)
    def _():
        cin[...] = jnp.zeros_like(cin)

    loads[0].wait()
    loads[1].wait()

    def state(h):
        wk = (column(tail_w, h) * k[:, cols(h)].astype(F32)).astype(BF16)
        return dot(wk, v[:, cols(h)], ((0,), (0,)))

    d_copy = remote(dec, pdec, d_send, d_recv, partner)
    e_copy = remote(cdec, odec, e_send, e_recv, across)

    def a_copy(a):
        part = st.at[0], rst.at[0]
        if a:
            some = pl.ds((a - 1) * (hq // 2), hq // 2)
            part = st.at[1, some], rst.at[1, some]
        return remote(*part, a_send.at[a], a_recv.at[a], partner)

    def x_copy(i):
        return remote(sx.at[i], rx.at[i], x_send.at[i], x_recv.at[i], across)

    def b_copy(i):
        return remote(cout.at[i], cin.at[i], b_send.at[i], b_recv.at[i], jnp.minimum(me + PLANE, n - 1))

    def y_copy(i):
        return remote(xs.at[i], xr.at[i], y_send.at[i], y_recv.at[i], across)

    def c_copy(a, i):
        return remote(cs.at[a, i], cr.at[a, i], c_send.at[a, i], c_recv.at[a, i], partner)

    def row(ref, h):
        return ref[pl.ds(h, 1), :]

    def states(to, a, far_core, lo, hi):
        def step(i, z):
            to[a, i] = state(head_of(a, far_core, i))
            return z
        lax.fori_loop(lo, hi, step, 0, unroll=hi - lo)

    def both(a, i):
        h = head_of(a, 0, i)
        mine, theirs = own[a, i], rst[a, i]
        early, late = jnp.where(first_core, mine, theirs), jnp.where(first_core, theirs, mine)
        return jnp.where(first_core, row(pdec, h), row(dec, h)) * early + late

    def across_step(i, z):
        sx[i] = both(1, i).astype(BF16)
        x_copy(i).start()
        return z

    hh = hq // 2
    states(st, 1, 1, 0, hh)
    pl.semaphore_wait(barrier, n - 1)
    d_copy.start()
    a_copy(1).start()
    states(st, 1, 1, hh, hq)
    a_copy(2).start()
    states(own, 1, 0, 0, hh)
    d_copy.wait_recv()
    cdec[...] = dec[...] * pdec[...]
    e_copy.start()
    states(own, 1, 0, hh, hq)
    a_copy(1).wait_recv()
    lax.fori_loop(0, hh, across_step, 0)
    states(st, 0, 1, 0, hh)
    a_copy(2).wait_recv()
    lax.fori_loop(hh, hq, across_step, 0)
    states(st, 0, 1, hh, hq)
    a_copy(0).start()
    states(own, 0, 0, 0, hh)
    states(own, 0, 0, hh, hq)
    experts = n
    ids = ids_ref[...]
    ex = lax.broadcasted_iota(jnp.int32, (experts, T), 0)
    first, second = (ids[0:1, :] == ex).astype(F32), (ids[1:2, :] == ex).astype(F32)
    earlier = dot((first + second).astype(BF16), (ti < si).astype(BF16))
    place = earlier + (ex * capp).astype(F32)
    row_of = [jnp.sum(one * place, axis=0, keepdims=True) for one in (first, second)]
    goal[0:1, :] = row_of[0]
    goal[1:2, :] = row_of[1]
    goal[2:8, :] = jnp.full((6, T), -1.0, F32)
    goal_copy = pltpu.make_async_remote_copy(
        goal, goal_in.at[land_slot], g_send, g_recv.at[land_slot],
        device_id={"ctx": lander}, device_id_type=pl.DeviceIdType.MESH)
    goal_copy.start()
    slot = lax.broadcasted_iota(jnp.int32, (half_n * capp, T), 0) + base * capp
    slot = slot.astype(F32)
    disp[0] = ((slot == row_of[0]) | (slot == row_of[1])).astype(BF16)

    a_copy(0).wait_recv()
    e_copy.wait_recv()

    def give(a, i, x):
        h = head_of(a, 0, i)
        after = (jnp.where(first_core, row(dec, h), row(pdec, h)) * x
                 + jnp.where(first_core, own[a, i], rst[a, i])).astype(BF16)
        x = x.astype(BF16)
        co[a, i] = jnp.where(first_core, x, after)
        cs[a, i] = jnp.where(first_core, after, x)
        c_copy(a, i).start()

    def scan_step(i):
        @pl.when(plane > 0)
        def _():
            b_copy(i).wait_recv()

        x_copy(i).wait_recv()
        h = head_of(0, 0, i)
        mine, theirs = both(0, i), rx[i].astype(F32)
        d_mine, d_theirs = row(cdec, h), row(odec, h)
        x = cin[i].astype(F32)
        mid = jnp.where(first_chip, d_mine, d_theirs) * x + jnp.where(first_chip, mine, theirs)
        last = jnp.where(first_chip, d_theirs, d_mine) * mid + jnp.where(first_chip, theirs, mine)
        cout[i] = last.astype(BF16)

        @pl.when(plane < planes - 1)
        def _():
            b_copy(i).start()

        xs[i] = jnp.where(first_chip, mid, x).astype(BF16)
        y_copy(i).start()
        give(0, i, jnp.where(first_chip, x, mid))

    def far_step(i):
        y_copy(i).wait_recv()
        give(1, i, xr[i].astype(F32))

    loads[2].wait()
    mask = ti >= si

    def intra_step(i):
        hs = [head_of(a, b, i) for a in range(2) for b in range(2)]
        scores = [dot(q[:, cols(h)], k[:, cols(h)], ((1,), (1,))) for h in hs]
        weights = [
            jnp.where(mask, x * jnp.exp(column(cum, h) - row(cum_t, h)), 0.0).astype(BF16)
            for x, h in zip(scores, hs)
        ]
        for w, h in zip(weights, hs):
            att[:, cols(h)] = dot(w, v[:, cols(h)])

    def gate_step(i):
        for j in range(PLANE):
            h = i * PLANE + j
            gated[:, cols(h)] = jax.nn.sigmoid(gate[:, cols(h)].astype(F32)) * again_ref[:, cols(h)]

    def inter_step(i):
        for a in range(2):
            c_copy(a, i).wait_recv()
        total = ss[...]
        for a in range(2):
            for b, carried in enumerate((co, cr)):
                h = head_of(a, b, i)
                x = att[:, cols(h)] + column(head_w, h) * dot(q[:, cols(h)], carried[a, i])
                att[:, cols(h)] = x
                total += x * x
        ss[...] = total

    ss[...] = jnp.zeros_like(ss)
    loads[3].wait()
    scan_at = START + HOP * plane
    far_at = jnp.maximum(scan_at + LAG, FAR)
    inter_at = far_at + LAG

    def during(i, at, step):
        @pl.when((i >= at) & (i < at + hq))
        def _():
            step(i - at)

    def mixed_step(i, z):
        during(i, scan_at, scan_step)
        during(i, far_at, far_step)
        during(i, 0, intra_step)
        during(i, hq, gate_step)
        during(i, inter_at, inter_step)
        return z

    lax.fori_loop(0, jnp.maximum(hq, inter_at) + hq, mixed_step, 0)

    rstd = lax.rsqrt(jnp.sum(ss[...], axis=1, keepdims=True) / D + 1e-6)
    loads[4].wait()
    ss[...] = jnp.zeros_like(ss)

    def branch_step(h, _):
        x = att[:, cols(h)] * rstd * gated[:, cols(h)]
        x = res[:, cols(h)].astype(F32) + x
        att[:, cols(h)] = x
        ss[...] += x * x
        return 0

    lax.fori_loop(0, heads, branch_step, 0, unroll=4)
    rstd2 = lax.rsqrt(jnp.sum(ss[...], axis=1, keepdims=True) / D + 1e-6)
    wide = D // PARTS

    def part(c):
        return pl.ds(pl.multiple_of(c * wide, wide), wide)

    def l_copy(c):
        return pltpu.make_async_remote_copy(
            normed.at[:, part(c)], landed.at[land_slot, :, part(c)], l_send.at[c], l_recv.at[land_slot, c],
            device_id={"ctx": lander}, device_id_type=pl.DeviceIdType.MESH)

    def norm_step(c, _):
        normed[:, part(c)] = (att[:, part(c)] * rstd2 * mgain_ref[:, part(c)]).astype(BF16)
        l_copy(c).start()
        return 0

    lax.fori_loop(0, PARTS, norm_step, 0)

    def near_step(c, _):
        rows = dot(disp[0], normed[:, part(c)]).astype(BF16)
        for e in range(half_n):
            near[e, :, part(c)] = rows[e * capp : e * capp + cap]
        return 0

    lax.fori_loop(0, PARTS, near_step, 0)

    def n_copy(j):
        e = (local + j) % half_n
        return pltpu.make_async_remote_copy(
            near.at[e], out_ref.at[me], n_send.at[j], n_recv.at[j],
            device_id={"ctx": base + e}, device_id_type=pl.DeviceIdType.MESH)

    keep = pltpu.make_async_copy(near.at[local], out_ref.at[me], n_send.at[0])
    keep.start()
    for j in range(1, half_n):
        n_copy(j).start()

    @pl.when(lands)
    def _():
        for x in range(2):
            pltpu.make_async_remote_copy(
                goal, goal_in.at[x], g_send, g_recv.at[x],
                device_id={"ctx": lander}, device_id_type=pl.DeviceIdType.MESH).wait_recv()
            disp[1 + x] = ((slot == goal_in[x, 0:1, :]) | (slot == goal_in[x, 1:2, :])).astype(BF16)

        def relay_step(s, _):
            x = jnp.where(s < PARTS, 1 - upper, upper)
            c = s % PARTS
            block = (far + x) * PLANE + rank
            at = block - (half_n - base)
            pltpu.make_async_remote_copy(
                normed.at[:, part(c)], landed.at[x, :, part(c)], l_send.at[c], l_recv.at[x, c],
                device_id={"ctx": lander}, device_id_type=pl.DeviceIdType.MESH).wait_recv()
            rows = dot(disp[1 + x], landed[x, :, part(c)]).astype(BF16)
            for e in range(half_n):
                relay[x, e, :, part(c)] = rows[e * capp : e * capp + cap]
            for j in range(1, half_n):
                e = (local + j) % half_n
                pltpu.make_async_remote_copy(
                    relay.at[x, e, :, part(c)], out_ref.at[block, :, part(c)],
                    r_send.at[x, j], r_recv.at[at],
                    device_id={"ctx": base + e}, device_id_type=pl.DeviceIdType.MESH).start()
            pltpu.make_async_copy(
                relay.at[x, local, :, part(c)], out_ref.at[block, :, part(c)], r_recv.at[at]).start()
            return 0

        lax.fori_loop(0, 2 * PARTS, relay_step, 0)
        for x in range(2):
            for j in range(1, half_n):
                pltpu.make_async_remote_copy(
                    relay.at[x, 0], out_ref.at[me], r_send.at[x, j], r_recv.at[0],
                    device_id={"ctx": lander}, device_id_type=pl.DeviceIdType.MESH).wait_send()

    keep.wait()
    for j in range(1, half_n):
        n_copy(j).wait()
    for b in range(half_n):
        pltpu.make_async_copy(near.at[0], out_ref.at[half_n - base + b], r_recv.at[b]).wait()
    lax.fori_loop(0, PARTS, lambda c, z: (l_copy(c).wait_send(), z)[1], 0)
    goal_copy.wait_send()
    d_copy.wait_send()
    e_copy.wait_send()
    for a in range(3):
        a_copy(a).wait_send()

    def sent(i, z):
        x_copy(i).wait_send()
        y_copy(i).wait_send()
        for a in range(2):
            c_copy(a, i).wait_send()
        return z

    lax.fori_loop(0, hq, sent, 0)

    @pl.when(plane < planes - 1)
    def _():
        lax.fori_loop(0, hq, lambda i, z: (b_copy(i).wait_send(), z)[1], 0)


def body(query, key_rows, value_rows, log_decay, gate_input, residual, attn_gain, moe_gain, expert_ids):
    T, D = query.shape
    heads = log_decay.shape[1]
    hd = D // heads
    n = lax.axis_size("ctx")
    experts = n
    cap = 5 * T * expert_ids.shape[1] // (4 * experts)
    hq = heads // PLANE
    capp = -(-cap // 16) * 16
    half_n = n // 2
    vm, anyspace = pl.BlockSpec(memory_space=pltpu.VMEM), pl.BlockSpec(memory_space=pl.ANY)
    V, DMA = pltpu.VMEM, pltpu.SemaphoreType.DMA
    arrived = pl.pallas_call(
        functools.partial(attend_kernel, (n, heads, hd, cap, capp)),
        out_shape=jax.ShapeDtypeStruct((n, cap, D), BF16),
        in_specs=[anyspace] * 3 + [vm] + [anyspace] * 2 + [vm] * 3,
        out_specs=anyspace,
        scratch_shapes=[
            V((T, D), BF16), V((T, D), BF16), V((T, D), BF16), V((T, D), BF16), V((T, D), BF16),
            V((T, D), F32), V((T, heads), F32), V((T, heads), F32), V((T, heads), F32), V((heads, T), F32), V((T, hd), F32),
            V((3, half_n * capp, T), BF16),
            V((heads, 128), F32), V((heads, 128), F32), V((heads, 128), F32), V((heads, 128), F32),
            V((2, hq, hd, hd), F32), V((2, hq, hd, hd), F32), V((2, hq, hd, hd), F32),
            V((hq, hd, hd), BF16), V((hq, hd, hd), BF16), V((hq, hd, hd), BF16), V((hq, hd, hd), BF16),
            V((hq, hd, hd), BF16), V((hq, hd, hd), BF16),
            V((2, hq, hd, hd), BF16), V((2, hq, hd, hd), BF16), V((2, hq, hd, hd), BF16),
            V((8, T), F32), V((2, 8, T), F32), V((T, D), F32), V((2, T, D), BF16),
            V((half_n, cap, D), BF16), V((2, half_n, cap, D), BF16),
            DMA((5,)), DMA, DMA, DMA, DMA, DMA((3,)), DMA((3,)), DMA((hq,)), DMA((hq,)), DMA((hq,)), DMA((hq,)),
            DMA((hq,)), DMA((hq,)), DMA((2, hq)), DMA((2, hq)),
            DMA, DMA((2,)), DMA((PARTS,)), DMA((2, PARTS)), DMA((half_n,)), DMA((half_n,)),
            DMA((2, half_n)), DMA((half_n,)),
        ],
        compiler_params=pltpu.CompilerParams(
            collective_id=0, has_side_effects=True, vmem_limit_bytes=67043328
        ),
        name="attend",
    )(
        query, key_rows, value_rows, log_decay.T, gate_input, residual,
        attn_gain.reshape(1, D), moe_gain.reshape(1, D), expert_ids.T,
    )
    return arrived.reshape(1, n * cap, D)


def solution(mesh):
    rows = P(("groups", "ctx"), None)
    return jax.shard_map(
        body, mesh=mesh, in_specs=(rows,) * 6 + (P(), P(), rows),
        out_specs=P(("groups", "ctx"), None, None), check_vma=False,
    )
```

```python
import functools

import jax
import jax.numpy as jnp
from jax import lax
from jax.experimental import pallas as pl
from jax.experimental.pallas import tpu as pltpu
from jax.sharding import PartitionSpec as P

PLANE = 4
START = 0
HOP = 3
LAG = 3
FAR = 11
PARTS = 24
F32 = jnp.float32
BF16 = jnp.bfloat16


def dot(a, b, dims=((1,), (0,)), precision=None):
    return lax.dot_general(a, b, (dims, ((), ())), preferred_element_type=F32, precision=precision)


def attend_kernel(
    sizes, q_hbm, k_hbm, v_hbm, ld_ref, gate_hbm, res_hbm, again_ref, mgain_ref, ids_ref, out_ref,
    q, k, v, gate, res, att, cum, tail_w, head_w, cum_t, ss, disp,
    dec, pdec, cdec, odec, own, st, rst, sx, rx, cin, cout, xs, xr, co, cs, cr,
    goal, goal_in, gated, landed, near, relay,
    in_sem, d_send, d_recv, e_send, e_recv, a_send, a_recv, x_send, x_recv, b_send, b_recv,
    y_send, y_recv, c_send, c_recv,
    g_send, g_recv, l_send, l_recv, n_send, n_recv, r_send, r_recv,
):
    n, heads, hd, cap, capp = sizes
    normed = k
    T, D = att.shape
    hq = heads // PLANE
    planes = n // PLANE
    me = lax.axis_index("ctx")
    plane, rank = me // PLANE, me % PLANE
    half_n = n // 2
    half_p = planes // 2
    upper = (plane >= half_p).astype(jnp.int32)
    base = upper * half_n
    local = me - base
    inner = jnp.where(upper == 1, plane - half_p, half_p - 1 - plane)
    outer = jnp.where(upper == 1, plane - half_p, plane)
    lander = jnp.where(upper == 1, half_p - 1 - outer // 2, half_p + outer // 2) * PLANE + rank
    land_slot = outer % 2
    lands = inner < half_p // 2
    far = jnp.minimum(2 * inner, half_p - 2) + (1 - upper) * half_p

    core, chip = rank % 2, rank // 2
    first_core, first_chip = core == 0, chip == 0
    partner = me + 1 - 2 * core
    across = me + 2 - 4 * chip

    def remote(src, dst, send, recv, to):
        return pltpu.make_async_remote_copy(
            src, dst, send, recv, device_id={"ctx": to}, device_id_type=pl.DeviceIdType.MESH)

    def head_of(far_chip, far_core, i):
        c = 1 - chip if far_chip else chip
        return (2 * c + (1 - core if far_core else core)) * hq + i

    loads = [
        pltpu.make_async_copy(s, t, in_sem.at[i])
        for i, (s, t) in enumerate(((k_hbm, k), (v_hbm, v), (q_hbm, q), (gate_hbm, gate), (res_hbm, res)))
    ]
    for load in loads:
        load.start()

    barrier = pltpu.get_barrier_semaphore()
    for d in range(1, n):
        pl.semaphore_signal(
            barrier, inc=1, device_id={"ctx": (me + d) % n}, device_id_type=pl.DeviceIdType.MESH)

    ti = lax.broadcasted_iota(jnp.int32, (T, T), 0)
    si = lax.broadcasted_iota(jnp.int32, (T, T), 1)
    ld = ld_ref[...]
    cum[...] = dot((ti >= si).astype(F32), ld, ((1,), (1,)), precision=lax.Precision.HIGHEST)
    tail_w[...] = jnp.exp(cum[T - 1 : T, :] - cum[...])
    head_w[...] = jnp.exp(cum[...])
    cum_t[...] = dot(ld, (ti <= si).astype(F32), precision=lax.Precision.HIGHEST)
    lane_head = lax.broadcasted_iota(jnp.int32, (T, heads), 1)

    def cols(h):
        return pl.ds(pl.multiple_of(h * hd, hd), hd)

    def column(ref, h):
        return jnp.sum(jnp.where(lane_head == h, ref[...], 0.0), axis=1, keepdims=True)

    dec[...] = jnp.broadcast_to(jnp.exp(cum_t[:, T - 1 : T]), dec.shape)

    @pl.when(plane == 0)
    def _():
        cin[...] = jnp.zeros_like(cin)

    loads[0].wait()
    loads[1].wait()

    def state(h):
        wk = (column(tail_w, h) * k[:, cols(h)].astype(F32)).astype(BF16)
        return dot(wk, v[:, cols(h)], ((0,), (0,)))

    d_copy = remote(dec, pdec, d_send, d_recv, partner)
    e_copy = remote(cdec, odec, e_send, e_recv, across)

    def a_copy(a):
        part = st.at[0], rst.at[0]
        if a:
            some = pl.ds((a - 1) * (hq // 2), hq // 2)
            part = st.at[1, some], rst.at[1, some]
        return remote(*part, a_send.at[a], a_recv.at[a], partner)

    def x_copy(i):
        return remote(sx.at[i], rx.at[i], x_send.at[i], x_recv.at[i], across)

    def b_copy(i):
        return remote(cout.at[i], cin.at[i], b_send.at[i], b_recv.at[i], jnp.minimum(me + PLANE, n - 1))

    def y_copy(i):
        return remote(xs.at[i], xr.at[i], y_send.at[i], y_recv.at[i], across)

    def c_copy(a, i):
        return remote(cs.at[a, i], cr.at[a, i], c_send.at[a, i], c_recv.at[a, i], partner)

    def row(ref, h):
        return ref[pl.ds(h, 1), :]

    def states(to, a, far_core, lo, hi):
        def step(i, z):
            to[a, i] = state(head_of(a, far_core, i))
            return z
        lax.fori_loop(lo, hi, step, 0, unroll=hi - lo)

    def both(a, i):
        h = head_of(a, 0, i)
        mine, theirs = own[a, i], rst[a, i]
        early, late = jnp.where(first_core, mine, theirs), jnp.where(first_core, theirs, mine)
        return jnp.where(first_core, row(pdec, h), row(dec, h)) * early + late

    def across_step(i, z):
        sx[i] = both(1, i).astype(BF16)
        x_copy(i).start()
        return z

    hh = hq // 2
    states(st, 1, 1, 0, hh)
    pl.semaphore_wait(barrier, n - 1)
    d_copy.start()
    a_copy(1).start()
    states(st, 1, 1, hh, hq)
    a_copy(2).start()
    states(own, 1, 0, 0, hh)
    d_copy.wait_recv()
    cdec[...] = dec[...] * pdec[...]
    e_copy.start()
    states(own, 1, 0, hh, hq)
    a_copy(1).wait_recv()
    lax.fori_loop(0, hh, across_step, 0)
    states(st, 0, 1, 0, hh)
    a_copy(2).wait_recv()
    lax.fori_loop(hh, hq, across_step, 0)
    states(st, 0, 1, hh, hq)
    a_copy(0).start()
    states(own, 0, 0, 0, hh)
    states(own, 0, 0, hh, hq)
    experts = n
    ids = ids_ref[...]
    ex = lax.broadcasted_iota(jnp.int32, (experts, T), 0)
    first, second = (ids[0:1, :] == ex).astype(F32), (ids[1:2, :] == ex).astype(F32)
    earlier = dot((first + second).astype(BF16), (ti < si).astype(BF16))
    place = earlier + (ex * capp).astype(F32)
    row_of = [jnp.sum(one * place, axis=0, keepdims=True) for one in (first, second)]
    goal[0:1, :] = row_of[0]
    goal[1:2, :] = row_of[1]
    goal[2:8, :] = jnp.full((6, T), -1.0, F32)
    goal_copy = pltpu.make_async_remote_copy(
        goal, goal_in.at[land_slot], g_send, g_recv.at[land_slot],
        device_id={"ctx": lander}, device_id_type=pl.DeviceIdType.MESH)
    goal_copy.start()
    slot = lax.broadcasted_iota(jnp.int32, (half_n * capp, T), 0) + base * capp
    slot = slot.astype(F32)
    disp[0] = ((slot == row_of[0]) | (slot == row_of[1])).astype(BF16)

    a_copy(0).wait_recv()
    e_copy.wait_recv()

    def give(a, i, x):
        h = head_of(a, 0, i)
        after = (jnp.where(first_core, row(dec, h), row(pdec, h)) * x
                 + jnp.where(first_core, own[a, i], rst[a, i])).astype(BF16)
        x = x.astype(BF16)
        co[a, i] = jnp.where(first_core, x, after)
        cs[a, i] = jnp.where(first_core, after, x)
        c_copy(a, i).start()

    def scan_step(i):
        @pl.when(plane > 0)
        def _():
            b_copy(i).wait_recv()

        x_copy(i).wait_recv()
        h = head_of(0, 0, i)
        mine, theirs = both(0, i), rx[i].astype(F32)
        d_mine, d_theirs = row(cdec, h), row(odec, h)
        x = cin[i].astype(F32)
        mid = jnp.where(first_chip, d_mine, d_theirs) * x + jnp.where(first_chip, mine, theirs)
        last = jnp.where(first_chip, d_theirs, d_mine) * mid + jnp.where(first_chip, theirs, mine)
        cout[i] = last.astype(BF16)

        @pl.when(plane < planes - 1)
        def _():
            b_copy(i).start()

        xs[i] = jnp.where(first_chip, mid, x).astype(BF16)
        y_copy(i).start()
        give(0, i, jnp.where(first_chip, x, mid))

    def far_step(i):
        y_copy(i).wait_recv()
        give(1, i, xr[i].astype(F32))

    loads[2].wait()
    mask = ti >= si

    def intra_step(i):
        hs = [head_of(a, b, i) for a in range(2) for b in range(2)]
        scores = [dot(q[:, cols(h)], k[:, cols(h)], ((1,), (1,))) for h in hs]
        weights = [
            jnp.where(mask, x * jnp.exp(column(cum, h) - row(cum_t, h)), 0.0).astype(BF16)
            for x, h in zip(scores, hs)
        ]
        for w, h in zip(weights, hs):
            att[:, cols(h)] = dot(w, v[:, cols(h)])

    def gate_step(i):
        for j in range(PLANE):
            h = i * PLANE + j
            gated[:, cols(h)] = jax.nn.sigmoid(gate[:, cols(h)].astype(F32)) * again_ref[:, cols(h)]

    def inter_step(i):
        for a in range(2):
            c_copy(a, i).wait_recv()
        total = ss[...]
        for a in range(2):
            for b, carried in enumerate((co, cr)):
                h = head_of(a, b, i)
                x = att[:, cols(h)] + column(head_w, h) * dot(q[:, cols(h)], carried[a, i])
                att[:, cols(h)] = x
                total += x * x
        ss[...] = total

    ss[...] = jnp.zeros_like(ss)
    loads[3].wait()
    scan_at = START + HOP * plane
    far_at = jnp.maximum(scan_at + LAG, FAR)
    inter_at = far_at + LAG

    def during(i, at, step):
        @pl.when((i >= at) & (i < at + hq))
        def _():
            step(i - at)

    def mixed_step(i, z):
        during(i, scan_at, scan_step)
        during(i, far_at, far_step)
        during(i, 0, intra_step)
        during(i, hq, gate_step)
        during(i, inter_at, inter_step)
        return z

    lax.fori_loop(0, jnp.maximum(hq, inter_at) + hq, mixed_step, 0)

    rstd = lax.rsqrt(jnp.sum(ss[...], axis=1, keepdims=True) / D + 1e-6)
    loads[4].wait()
    ss[...] = jnp.zeros_like(ss)

    def branch_step(h, _):
        x = att[:, cols(h)] * rstd * gated[:, cols(h)]
        x = res[:, cols(h)].astype(F32) + x
        att[:, cols(h)] = x
        ss[...] += x * x
        return 0

    lax.fori_loop(0, heads, branch_step, 0, unroll=4)
    rstd2 = lax.rsqrt(jnp.sum(ss[...], axis=1, keepdims=True) / D + 1e-6)
    wide = D // PARTS

    def part(c):
        return pl.ds(pl.multiple_of(c * wide, wide), wide)

    def l_copy(c):
        return pltpu.make_async_remote_copy(
            normed.at[:, part(c)], landed.at[land_slot, :, part(c)], l_send.at[c], l_recv.at[land_slot, c],
            device_id={"ctx": lander}, device_id_type=pl.DeviceIdType.MESH)

    def norm_step(c, _):
        normed[:, part(c)] = (att[:, part(c)] * rstd2 * mgain_ref[:, part(c)]).astype(BF16)
        l_copy(c).start()
        return 0

    lax.fori_loop(0, PARTS, norm_step, 0)

    def near_step(c, _):
        rows = dot(disp[0], normed[:, part(c)]).astype(BF16)
        for e in range(half_n):
            near[e, :, part(c)] = rows[e * capp : e * capp + cap]
        return 0

    lax.fori_loop(0, PARTS, near_step, 0)

    def n_copy(j):
        e = (local + j) % half_n
        return pltpu.make_async_remote_copy(
            near.at[e], out_ref.at[me], n_send.at[j], n_recv.at[j],
            device_id={"ctx": base + e}, device_id_type=pl.DeviceIdType.MESH)

    keep = pltpu.make_async_copy(near.at[local], out_ref.at[me], n_send.at[0])
    keep.start()
    for j in range(1, half_n):
        n_copy(j).start()

    @pl.when(lands)
    def _():
        for x in range(2):
            pltpu.make_async_remote_copy(
                goal, goal_in.at[x], g_send, g_recv.at[x],
                device_id={"ctx": lander}, device_id_type=pl.DeviceIdType.MESH).wait_recv()
            disp[1 + x] = ((slot == goal_in[x, 0:1, :]) | (slot == goal_in[x, 1:2, :])).astype(BF16)

        def relayed(c):
            return remote(relay.at[:, :, part(c)], relay.at[:, :, part(c)], r_send.at[c], r_recv.at[0], lander)

        def relay_step(s, _):
            x = jnp.where(s < PARTS, 1 - upper, upper)
            c = s % PARTS
            block = (far + x) * PLANE + rank
            at = block - (half_n - base)

            @pl.when(s >= PARTS)
            def _():
                relayed(c).wait_send()

            pltpu.make_async_remote_copy(
                normed.at[:, part(c)], landed.at[x, :, part(c)], l_send.at[c], l_recv.at[x, c],
                device_id={"ctx": lander}, device_id_type=pl.DeviceIdType.MESH).wait_recv()
            rows = dot(disp[1 + x], landed[x, :, part(c)]).astype(BF16)
            for e in range(half_n):
                relay[e, :, part(c)] = rows[e * capp : e * capp + cap]
            for j in range(1, half_n):
                e = (local + j) % half_n
                remote(relay.at[e, :, part(c)], out_ref.at[block, :, part(c)],
                       r_send.at[c], r_recv.at[at], base + e).start()
            pltpu.make_async_copy(
                relay.at[local, :, part(c)], out_ref.at[block, :, part(c)], r_send.at[c]).start()
            return 0

        lax.fori_loop(0, 2 * PARTS, relay_step, 0)
        lax.fori_loop(0, PARTS, lambda c, z: (relayed(c).wait_send(), z)[1], 0)

    keep.wait()
    for j in range(1, half_n):
        n_copy(j).wait()
    first = far * PLANE + rank - (half_n - base)
    for b in range(half_n):
        @pl.when(jnp.logical_not(lands & ((b == first) | (b == first + PLANE))))
        def _():
            pltpu.make_async_copy(near.at[0], out_ref.at[half_n - base + b], r_recv.at[b]).wait()
    lax.fori_loop(0, PARTS, lambda c, z: (l_copy(c).wait_send(), z)[1], 0)
    goal_copy.wait_send()
    d_copy.wait_send()
    e_copy.wait_send()
    for a in range(3):
        a_copy(a).wait_send()

    def sent(i, z):
        x_copy(i).wait_send()
        y_copy(i).wait_send()
        for a in range(2):
            c_copy(a, i).wait_send()
        return z

    lax.fori_loop(0, hq, sent, 0)

    @pl.when(plane < planes - 1)
    def _():
        lax.fori_loop(0, hq, lambda i, z: (b_copy(i).wait_send(), z)[1], 0)


def body(query, key_rows, value_rows, log_decay, gate_input, residual, attn_gain, moe_gain, expert_ids):
    T, D = query.shape
    heads = log_decay.shape[1]
    hd = D // heads
    n = lax.axis_size("ctx")
    experts = n
    cap = 5 * T * expert_ids.shape[1] // (4 * experts)
    hq = heads // PLANE
    capp = -(-cap // 16) * 16
    half_n = n // 2
    vm, anyspace = pl.BlockSpec(memory_space=pltpu.VMEM), pl.BlockSpec(memory_space=pl.ANY)
    V, DMA = pltpu.VMEM, pltpu.SemaphoreType.DMA
    arrived = pl.pallas_call(
        functools.partial(attend_kernel, (n, heads, hd, cap, capp)),
        out_shape=pltpu.VMEM((n, cap, D), BF16),
        in_specs=[anyspace] * 3 + [vm] + [anyspace] * 2 + [vm] * 3,
        out_specs=anyspace,
        scratch_shapes=[
            V((T, D), BF16), V((T, D), BF16), V((T, D), BF16), V((T, D), BF16), V((T, D), BF16),
            V((T, D), F32), V((T, heads), F32), V((T, heads), F32), V((T, heads), F32), V((heads, T), F32), V((T, hd), F32),
            V((3, half_n * capp, T), BF16),
            V((heads, 128), F32), V((heads, 128), F32), V((heads, 128), F32), V((heads, 128), F32),
            V((2, hq, hd, hd), F32), V((2, hq, hd, hd), F32), V((2, hq, hd, hd), F32),
            V((hq, hd, hd), BF16), V((hq, hd, hd), BF16), V((hq, hd, hd), BF16), V((hq, hd, hd), BF16),
            V((hq, hd, hd), BF16), V((hq, hd, hd), BF16),
            V((2, hq, hd, hd), BF16), V((2, hq, hd, hd), BF16), V((2, hq, hd, hd), BF16),
            V((8, T), F32), V((2, 8, T), F32), V((T, D), F32), V((2, T, D), BF16),
            V((half_n, cap, D), BF16), V((half_n, cap, D), BF16),
            DMA((5,)), DMA, DMA, DMA, DMA, DMA((3,)), DMA((3,)), DMA((hq,)), DMA((hq,)), DMA((hq,)), DMA((hq,)),
            DMA((hq,)), DMA((hq,)), DMA((2, hq)), DMA((2, hq)),
            DMA, DMA((2,)), DMA((PARTS,)), DMA((2, PARTS)), DMA((half_n,)), DMA((half_n,)),
            DMA((PARTS,)), DMA((half_n,)),
        ],
        compiler_params=pltpu.CompilerParams(
            collective_id=0, has_side_effects=True, vmem_limit_bytes=57000000
        ),
        name="attend",
    )(
        query, key_rows, value_rows, log_decay.T, gate_input, residual,
        attn_gain.reshape(1, D), moe_gain.reshape(1, D), expert_ids.T,
    )
    return arrived.reshape(1, n * cap, D)


def solution(mesh):
    rows = P(("groups", "ctx"), None)
    return jax.shard_map(
        body, mesh=mesh, in_specs=(rows,) * 6 + (P(), P(), rows),
        out_specs=P(("groups", "ctx"), None, None), check_vma=False,
    )
```

```python
import functools

import jax
import jax.numpy as jnp
from jax import lax
from jax.experimental import pallas as pl
from jax.experimental.pallas import tpu as pltpu
from jax.sharding import PartitionSpec as P

PLANE = 4
START = 0
HOP = 3
LAG = 3
FAR = 11
GAP = 2
PARTS = 24
F32 = jnp.float32
BF16 = jnp.bfloat16


def dot(a, b, dims=((1,), (0,)), precision=None):
    return lax.dot_general(a, b, (dims, ((), ())), preferred_element_type=F32, precision=precision)


def attend_kernel(
    sizes, q_hbm, k_hbm, v_hbm, ld_ref, gate_hbm, res_hbm, again_ref, mgain_ref, ids_ref, out_ref,
    q, k, v, gate, res, att, cum, tail_w, head_w, cum_t, ss, disp,
    dec, pdec, cdec, odec, own, st, rst, sx, rx, cin, cout, xs, xr, co, cs, cr,
    goal, goal_in, gated, landed, near, relay,
    in_sem, d_send, d_recv, e_send, e_recv, a_send, a_recv, x_send, x_recv, b_send, b_recv,
    y_send, y_recv, c_send, c_recv,
    g_send, g_recv, l_send, l_recv, n_send, n_recv, r_send, r_recv, column_in, across_in, partner_in,
):
    n, heads, hd, cap, capp = sizes
    normed = k
    T, D = att.shape
    hq = heads // PLANE
    planes = n // PLANE
    me = lax.axis_index("ctx")
    plane, rank = me // PLANE, me % PLANE
    half_n = n // 2
    half_p = planes // 2
    upper = (plane >= half_p).astype(jnp.int32)
    base = upper * half_n
    local = me - base
    inner = jnp.where(upper == 1, plane - half_p, half_p - 1 - plane)
    outer = jnp.where(upper == 1, plane - half_p, plane)
    lander = jnp.where(upper == 1, half_p - 1 - outer // 2, half_p + outer // 2) * PLANE + rank
    land_slot = outer % 2
    lands = inner < half_p // 2
    far = jnp.minimum(2 * inner, half_p - 2) + (1 - upper) * half_p

    core, chip = rank % 2, rank // 2
    first_core, first_chip = core == 0, chip == 0
    partner = me + 1 - 2 * core
    across = me + 2 - 4 * chip

    def remote(src, dst, send, recv, to):
        return pltpu.make_async_remote_copy(
            src, dst, send, recv, device_id={"ctx": to}, device_id_type=pl.DeviceIdType.MESH)

    def head_of(far_chip, far_core, i):
        c = 1 - chip if far_chip else chip
        return (2 * c + (1 - core if far_core else core)) * hq + i

    quarters = [(1, 1), (1, 0), (0, 1), (0, 0)]

    def quarter_load(i):
        at = pl.ds(pl.multiple_of(head_of(*quarters[i], 0) * hd, hd), hq * hd)
        return [
            pltpu.make_async_copy(src.at[:, at], dst.at[:, at], in_sem.at[2 * i + j])
            for j, (src, dst) in enumerate(((k_hbm, k), (v_hbm, v)))
        ]

    def start_quarter(i):
        for load in quarter_load(i):
            load.start()

    def wait_quarter(i):
        for load in quarter_load(i):
            load.wait()

    q_load, gate_load, res_load = (
        pltpu.make_async_copy(src, dst, in_sem.at[8 + i])
        for i, (src, dst) in enumerate(((q_hbm, q), (gate_hbm, gate), (res_hbm, res)))
    )
    start_quarter(0)
    start_quarter(1)

    barrier = pltpu.get_barrier_semaphore()

    def tell(sem, to):
        pl.semaphore_signal(sem, inc=1, device_id={"ctx": to}, device_id_type=pl.DeviceIdType.MESH)

    def tell_column(sem):
        @pl.when(plane > 0)
        def _():
            tell(sem, me - PLANE)

        @pl.when(plane < planes - 1)
        def _():
            tell(sem, me + PLANE)

    beside = (plane > 0).astype(jnp.int32) + (plane < planes - 1).astype(jnp.int32)
    tell(barrier, partner)
    tell(barrier, across)
    tell_column(barrier)

    ti = lax.broadcasted_iota(jnp.int32, (T, T), 0)
    si = lax.broadcasted_iota(jnp.int32, (T, T), 1)
    ld = ld_ref[...]
    cum[...] = dot((ti >= si).astype(F32), ld, ((1,), (1,)), precision=lax.Precision.HIGHEST)
    tail_w[...] = jnp.exp(cum[T - 1 : T, :] - cum[...])
    head_w[...] = jnp.exp(cum[...])
    cum_t[...] = dot(ld, (ti <= si).astype(F32), precision=lax.Precision.HIGHEST)
    lane_head = lax.broadcasted_iota(jnp.int32, (T, heads), 1)

    def cols(h):
        return pl.ds(pl.multiple_of(h * hd, hd), hd)

    def column(ref, h):
        return jnp.sum(jnp.where(lane_head == h, ref[...], 0.0), axis=1, keepdims=True)

    dec[...] = jnp.broadcast_to(jnp.exp(cum_t[:, T - 1 : T]), dec.shape)

    @pl.when(plane == 0)
    def _():
        cin[...] = jnp.zeros_like(cin)

    def state(h):
        wk = (column(tail_w, h) * k[:, cols(h)].astype(F32)).astype(BF16)
        return dot(wk, v[:, cols(h)], ((0,), (0,)))

    d_copy = remote(dec, pdec, d_send, d_recv, partner)
    e_copy = remote(cdec, odec, e_send, e_recv, across)

    def a_copy(a):
        part = st.at[0], rst.at[0]
        if a:
            some = pl.ds((a - 1) * (hq // 2), hq // 2)
            part = st.at[1, some], rst.at[1, some]
        return remote(*part, a_send.at[a], a_recv.at[a], partner)

    def x_copy(i):
        return remote(sx.at[i], rx.at[i], x_send.at[i], x_recv.at[i], across)

    def b_copy(i):
        return remote(cout.at[i], cin.at[i], b_send.at[i], b_recv.at[i], jnp.minimum(me + PLANE, n - 1))

    def y_copy(i):
        return remote(xs.at[i], xr.at[i], y_send.at[i], y_recv.at[i], across)

    def c_copy(a, i):
        return remote(cs.at[a, i], cr.at[a, i], c_send.at[a, i], c_recv.at[a, i], partner)

    def row(ref, h):
        return ref[pl.ds(h, 1), :]

    def states(to, a, far_core, lo, hi):
        def step(i, z):
            to[a, i] = state(head_of(a, far_core, i))
            return z
        lax.fori_loop(lo, hi, step, 0, unroll=hi - lo)

    def both(a, i):
        h = head_of(a, 0, i)
        mine, theirs = own[a, i], rst[a, i]
        early, late = jnp.where(first_core, mine, theirs), jnp.where(first_core, theirs, mine)
        return jnp.where(first_core, row(pdec, h), row(dec, h)) * early + late

    def across_step(i, z):
        sx[i] = both(1, i).astype(BF16)
        x_copy(i).start()
        return z

    hh = hq // 2
    experts = n
    ids = ids_ref[...]
    ex = lax.broadcasted_iota(jnp.int32, (experts, T), 0)
    first, second = (ids[0:1, :] == ex).astype(F32), (ids[1:2, :] == ex).astype(F32)
    earlier = dot((first + second).astype(BF16), (ti < si).astype(BF16))
    place = earlier + (ex * capp).astype(F32)
    row_of = [jnp.sum(one * place, axis=0, keepdims=True) for one in (first, second)]
    goal[0:1, :] = row_of[0]
    goal[1:2, :] = row_of[1]
    goal[2:8, :] = jnp.full((6, T), -1.0, F32)
    goal_copy = pltpu.make_async_remote_copy(
        goal, goal_in.at[land_slot], g_send, g_recv.at[land_slot],
        device_id={"ctx": lander}, device_id_type=pl.DeviceIdType.MESH)
    slot = lax.broadcasted_iota(jnp.int32, (half_n * capp, T), 0) + base * capp
    slot = slot.astype(F32)
    disp[0] = ((slot == row_of[0]) | (slot == row_of[1])).astype(BF16)

    wait_quarter(0)
    start_quarter(2)
    states(st, 1, 1, 0, hh)
    pl.semaphore_wait(barrier, 2 + beside)
    tell_column(column_in.at[0])
    d_copy.start()
    a_copy(1).start()
    states(st, 1, 1, hh, hq)
    a_copy(2).start()
    wait_quarter(1)
    start_quarter(3)
    q_load.start()
    states(own, 1, 0, 0, hh)
    d_copy.wait_recv()
    cdec[...] = dec[...] * pdec[...]
    e_copy.start()
    states(own, 1, 0, hh, hq)
    a_copy(1).wait_recv()
    lax.fori_loop(0, hh, across_step, 0)
    wait_quarter(2)
    gate_load.start()
    states(st, 0, 1, 0, hh)
    a_copy(2).wait_recv()
    lax.fori_loop(hh, hq, across_step, 0)
    states(st, 0, 1, hh, hq)
    a_copy(0).start()
    wait_quarter(3)
    res_load.start()
    states(own, 0, 0, 0, hh)
    states(own, 0, 0, hh, hq)
    a_copy(0).wait_recv()
    e_copy.wait_recv()

    def give(a, i, x):
        h = head_of(a, 0, i)
        after = (jnp.where(first_core, row(dec, h), row(pdec, h)) * x
                 + jnp.where(first_core, own[a, i], rst[a, i])).astype(BF16)
        x = x.astype(BF16)
        co[a, i] = jnp.where(first_core, x, after)
        cs[a, i] = jnp.where(first_core, after, x)
        c_copy(a, i).start()

    def scan_step(i):
        @pl.when(plane > 0)
        def _():
            b_copy(i).wait_recv()

        x_copy(i).wait_recv()
        h = head_of(0, 0, i)
        mine, theirs = both(0, i), rx[i].astype(F32)
        d_mine, d_theirs = row(cdec, h), row(odec, h)
        x = cin[i].astype(F32)
        mid = jnp.where(first_chip, d_mine, d_theirs) * x + jnp.where(first_chip, mine, theirs)
        last = jnp.where(first_chip, d_theirs, d_mine) * mid + jnp.where(first_chip, theirs, mine)
        cout[i] = last.astype(BF16)

        @pl.when(plane < planes - 1)
        def _():
            b_copy(i).start()

        xs[i] = jnp.where(first_chip, mid, x).astype(BF16)
        y_copy(i).start()
        give(0, i, jnp.where(first_chip, x, mid))

    def far_step(i):
        y_copy(i).wait_recv()
        give(1, i, xr[i].astype(F32))

    q_load.wait()
    mask = ti >= si

    def intra_step(i):
        hs = [head_of(a, b, i) for a in range(2) for b in range(2)]
        scores = [dot(q[:, cols(h)], k[:, cols(h)], ((1,), (1,))) for h in hs]
        weights = [
            jnp.where(mask, x * jnp.exp(column(cum, h) - row(cum_t, h)), 0.0).astype(BF16)
            for x, h in zip(scores, hs)
        ]
        for w, h in zip(weights, hs):
            att[:, cols(h)] = dot(w, v[:, cols(h)])

    def gate_step(i):
        for j in range(PLANE):
            h = i * PLANE + j
            gated[:, cols(h)] = jax.nn.sigmoid(gate[:, cols(h)].astype(F32)) * again_ref[:, cols(h)]

    def inter_step(i):
        for a in range(2):
            c_copy(a, i).wait_recv()
        total = ss[...]
        for a in range(2):
            for b, carried in enumerate((co, cr)):
                h = head_of(a, b, i)
                x = att[:, cols(h)] + column(head_w, h) * dot(q[:, cols(h)], carried[a, i])
                att[:, cols(h)] = x
                total += x * x
        ss[...] = total

    ss[...] = jnp.zeros_like(ss)
    gate_load.wait()
    scan_at = START + HOP * plane
    far_at = jnp.maximum(scan_at + LAG, FAR)
    inter_at = far_at + LAG

    def during(i, at, step):
        @pl.when((i >= at) & (i < at + hq))
        def _():
            step(i - at)

    def meet(i):
        for r in range(planes):
            @pl.when(i == (r + 1) * GAP)
            def _():
                if r < planes - 2:
                    pl.semaphore_wait(column_in.at[r], beside)
                if r < planes - 3:
                    tell_column(column_in.at[r + 1])
                if r == planes - 3:
                    tell(across_in, across)
                if r == planes - 2:
                    pl.semaphore_wait(across_in, 1)
                    tell(partner_in, partner)
                if r == planes - 1:
                    pl.semaphore_wait(partner_in, 1)
                    goal_copy.start()

    def mixed_step(i, z):
        meet(i)
        during(i, scan_at, scan_step)
        during(i, far_at, far_step)
        during(i, 0, intra_step)
        during(i, hq, gate_step)
        during(i, inter_at, inter_step)
        return z

    lax.fori_loop(0, jnp.maximum(hq, inter_at) + hq, mixed_step, 0)

    rstd = lax.rsqrt(jnp.sum(ss[...], axis=1, keepdims=True) / D + 1e-6)
    res_load.wait()
    ss[...] = jnp.zeros_like(ss)

    def branch_step(h, _):
        x = att[:, cols(h)] * rstd * gated[:, cols(h)]
        x = res[:, cols(h)].astype(F32) + x
        att[:, cols(h)] = x
        ss[...] += x * x
        return 0

    lax.fori_loop(0, heads, branch_step, 0, unroll=4)
    rstd2 = lax.rsqrt(jnp.sum(ss[...], axis=1, keepdims=True) / D + 1e-6)
    wide = D // PARTS

    def part(c):
        return pl.ds(pl.multiple_of(c * wide, wide), wide)

    def l_copy(c):
        return pltpu.make_async_remote_copy(
            normed.at[:, part(c)], landed.at[land_slot, :, part(c)], l_send.at[c], l_recv.at[land_slot, c],
            device_id={"ctx": lander}, device_id_type=pl.DeviceIdType.MESH)

    def norm_step(c, _):
        normed[:, part(c)] = (att[:, part(c)] * rstd2 * mgain_ref[:, part(c)]).astype(BF16)
        l_copy(c).start()
        return 0

    lax.fori_loop(0, PARTS, norm_step, 0)

    def near_step(c, _):
        rows = dot(disp[0], normed[:, part(c)]).astype(BF16)
        for e in range(half_n):
            near[e, :, part(c)] = rows[e * capp : e * capp + cap]
        return 0

    lax.fori_loop(0, PARTS, near_step, 0)

    def n_copy(j):
        e = (local + j) % half_n
        return pltpu.make_async_remote_copy(
            near.at[e], out_ref.at[me], n_send.at[j], n_recv.at[j],
            device_id={"ctx": base + e}, device_id_type=pl.DeviceIdType.MESH)

    keep = pltpu.make_async_copy(near.at[local], out_ref.at[me], n_send.at[0])
    keep.start()
    for j in range(1, half_n):
        n_copy(j).start()

    @pl.when(lands)
    def _():
        for x in range(2):
            pltpu.make_async_remote_copy(
                goal, goal_in.at[x], g_send, g_recv.at[x],
                device_id={"ctx": lander}, device_id_type=pl.DeviceIdType.MESH).wait_recv()
            disp[1 + x] = ((slot == goal_in[x, 0:1, :]) | (slot == goal_in[x, 1:2, :])).astype(BF16)

        def relayed(c):
            return remote(relay.at[:, :, part(c)], relay.at[:, :, part(c)], r_send.at[c], r_recv.at[0], lander)

        def relay_step(s, _):
            x = jnp.where(s < PARTS, 1 - upper, upper)
            c = s % PARTS
            block = (far + x) * PLANE + rank
            at = block - (half_n - base)

            @pl.when(s >= PARTS)
            def _():
                relayed(c).wait_send()

            pltpu.make_async_remote_copy(
                normed.at[:, part(c)], landed.at[x, :, part(c)], l_send.at[c], l_recv.at[x, c],
                device_id={"ctx": lander}, device_id_type=pl.DeviceIdType.MESH).wait_recv()
            rows = dot(disp[1 + x], landed[x, :, part(c)]).astype(BF16)
            for e in range(half_n):
                relay[e, :, part(c)] = rows[e * capp : e * capp + cap]
            for j in range(1, half_n):
                e = (local + j) % half_n
                remote(relay.at[e, :, part(c)], out_ref.at[block, :, part(c)],
                       r_send.at[c], r_recv.at[at], base + e).start()
            pltpu.make_async_copy(
                relay.at[local, :, part(c)], out_ref.at[block, :, part(c)], r_send.at[c]).start()
            return 0

        lax.fori_loop(0, 2 * PARTS, relay_step, 0)
        lax.fori_loop(0, PARTS, lambda c, z: (relayed(c).wait_send(), z)[1], 0)

    keep.wait()
    for j in range(1, half_n):
        n_copy(j).wait()
    first = far * PLANE + rank - (half_n - base)
    for b in range(half_n):
        @pl.when(jnp.logical_not(lands & ((b == first) | (b == first + PLANE))))
        def _():
            pltpu.make_async_copy(near.at[0], out_ref.at[half_n - base + b], r_recv.at[b]).wait()
    lax.fori_loop(0, PARTS, lambda c, z: (l_copy(c).wait_send(), z)[1], 0)
    goal_copy.wait_send()
    d_copy.wait_send()
    e_copy.wait_send()
    for a in range(3):
        a_copy(a).wait_send()

    def sent(i, z):
        x_copy(i).wait_send()
        y_copy(i).wait_send()
        for a in range(2):
            c_copy(a, i).wait_send()
        return z

    lax.fori_loop(0, hq, sent, 0)

    @pl.when(plane < planes - 1)
    def _():
        lax.fori_loop(0, hq, lambda i, z: (b_copy(i).wait_send(), z)[1], 0)


def body(query, key_rows, value_rows, log_decay, gate_input, residual, attn_gain, moe_gain, expert_ids):
    T, D = query.shape
    heads = log_decay.shape[1]
    hd = D // heads
    n = lax.axis_size("ctx")
    experts = n
    cap = 5 * T * expert_ids.shape[1] // (4 * experts)
    hq = heads // PLANE
    capp = -(-cap // 16) * 16
    half_n = n // 2
    vm, anyspace = pl.BlockSpec(memory_space=pltpu.VMEM), pl.BlockSpec(memory_space=pl.ANY)
    V, DMA, REG = pltpu.VMEM, pltpu.SemaphoreType.DMA, pltpu.SemaphoreType.REGULAR
    arrived = pl.pallas_call(
        functools.partial(attend_kernel, (n, heads, hd, cap, capp)),
        out_shape=pltpu.VMEM((n, cap, D), BF16),
        in_specs=[anyspace] * 3 + [vm] + [anyspace] * 2 + [vm] * 3,
        out_specs=anyspace,
        scratch_shapes=[
            V((T, D), BF16), V((T, D), BF16), V((T, D), BF16), V((T, D), BF16), V((T, D), BF16),
            V((T, D), F32), V((T, heads), F32), V((T, heads), F32), V((T, heads), F32), V((heads, T), F32), V((T, hd), F32),
            V((3, half_n * capp, T), BF16),
            V((heads, 128), F32), V((heads, 128), F32), V((heads, 128), F32), V((heads, 128), F32),
            V((2, hq, hd, hd), F32), V((2, hq, hd, hd), F32), V((2, hq, hd, hd), F32),
            V((hq, hd, hd), BF16), V((hq, hd, hd), BF16), V((hq, hd, hd), BF16), V((hq, hd, hd), BF16),
            V((hq, hd, hd), BF16), V((hq, hd, hd), BF16),
            V((2, hq, hd, hd), BF16), V((2, hq, hd, hd), BF16), V((2, hq, hd, hd), BF16),
            V((8, T), F32), V((2, 8, T), F32), V((T, D), F32), V((2, T, D), BF16),
            V((half_n, cap, D), BF16), V((half_n, cap, D), BF16),
            DMA((11,)), DMA, DMA, DMA, DMA, DMA((3,)), DMA((3,)), DMA((hq,)), DMA((hq,)), DMA((hq,)), DMA((hq,)),
            DMA((hq,)), DMA((hq,)), DMA((2, hq)), DMA((2, hq)),
            DMA, DMA((2,)), DMA((PARTS,)), DMA((2, PARTS)), DMA((half_n,)), DMA((half_n,)),
            DMA((PARTS,)), DMA((half_n,)), REG((n // PLANE - 2,)), REG, REG,
        ],
        compiler_params=pltpu.CompilerParams(
            collective_id=0, has_side_effects=True, vmem_limit_bytes=57000000
        ),
        name="attend",
    )(
        query, key_rows, value_rows, log_decay.T, gate_input, residual,
        attn_gain.reshape(1, D), moe_gain.reshape(1, D), expert_ids.T,
    )
    return arrived.reshape(1, n * cap, D)


def solution(mesh):
    rows = P(("groups", "ctx"), None)
    return jax.shard_map(
        body, mesh=mesh, in_specs=(rows,) * 6 + (P(), P(), rows),
        out_specs=P(("groups", "ctx"), None, None), check_vma=False,
    )
```

```python
import functools

import jax
import jax.numpy as jnp
from jax import lax
from jax.experimental import pallas as pl
from jax.experimental.pallas import tpu as pltpu
from jax.sharding import PartitionSpec as P

PLANE = 4
START = 0
HOP = 3
LAG = 3
FAR = 11
GAP = 2
BRANCH = 4
PARTS = 24
F32 = jnp.float32
BF16 = jnp.bfloat16


def dot(a, b, dims=((1,), (0,)), precision=None):
    return lax.dot_general(a, b, (dims, ((), ())), preferred_element_type=F32, precision=precision)


def attend_kernel(
    sizes, q_hbm, k_hbm, v_hbm, ld_ref, gate_hbm, res_hbm, again_ref, mgain_ref, ids_ref, out_ref,
    q, k, v, gate, res, att, cum, tail_w, head_w, cum_t, ss, disp,
    dec, pdec, cdec, odec, own, st, rst, sx, rx, cin, cout, xs, xr, co, cs, cr,
    goal, goal_in, gated, landed, near, relay,
    in_sem, d_send, d_recv, e_send, e_recv, a_send, a_recv, x_send, x_recv, b_send, b_recv,
    y_send, y_recv, c_send, c_recv,
    g_send, g_recv, l_send, l_recv, n_send, n_recv, r_send, r_recv, column_in, across_in, partner_in,
):
    n, heads, hd, cap, capp = sizes
    normed = k
    T, D = att.shape
    hq = heads // PLANE
    planes = n // PLANE
    me = lax.axis_index("ctx")
    plane, rank = me // PLANE, me % PLANE
    half_n = n // 2
    half_p = planes // 2
    upper = (plane >= half_p).astype(jnp.int32)
    base = upper * half_n
    local = me - base
    inner = jnp.where(upper == 1, plane - half_p, half_p - 1 - plane)
    outer = jnp.where(upper == 1, plane - half_p, plane)
    lander = jnp.where(upper == 1, half_p - 1 - outer // 2, half_p + outer // 2) * PLANE + rank
    land_slot = outer % 2
    lands = inner < half_p // 2
    far = jnp.minimum(2 * inner, half_p - 2) + (1 - upper) * half_p

    core, chip = rank % 2, rank // 2
    first_core, first_chip = core == 0, chip == 0
    partner = me + 1 - 2 * core
    across = me + 2 - 4 * chip

    def remote(src, dst, send, recv, to):
        return pltpu.make_async_remote_copy(
            src, dst, send, recv, device_id={"ctx": to}, device_id_type=pl.DeviceIdType.MESH)

    def head_of(far_chip, far_core, i):
        c = 1 - chip if far_chip else chip
        return (2 * c + (1 - core if far_core else core)) * hq + i

    quarters = [(1, 1), (1, 0), (0, 1), (0, 0)]

    def quarter_load(i):
        at = pl.ds(pl.multiple_of(head_of(*quarters[i], 0) * hd, hd), hq * hd)
        return [
            pltpu.make_async_copy(src.at[:, at], dst.at[:, at], in_sem.at[2 * i + j])
            for j, (src, dst) in enumerate(((k_hbm, k), (v_hbm, v)))
        ]

    def start_quarter(i):
        for load in quarter_load(i):
            load.start()

    def wait_quarter(i):
        for load in quarter_load(i):
            load.wait()

    q_load, gate_load, res_load = (
        pltpu.make_async_copy(src, dst, in_sem.at[8 + i])
        for i, (src, dst) in enumerate(((q_hbm, q), (gate_hbm, gate), (res_hbm, res)))
    )
    start_quarter(0)
    start_quarter(1)

    barrier = pltpu.get_barrier_semaphore()

    def tell(sem, to):
        pl.semaphore_signal(sem, inc=1, device_id={"ctx": to}, device_id_type=pl.DeviceIdType.MESH)

    def tell_column(sem):
        @pl.when(plane > 0)
        def _():
            tell(sem, me - PLANE)

        @pl.when(plane < planes - 1)
        def _():
            tell(sem, me + PLANE)

    beside = (plane > 0).astype(jnp.int32) + (plane < planes - 1).astype(jnp.int32)
    tell(barrier, partner)
    tell(barrier, across)
    tell_column(barrier)

    ti = lax.broadcasted_iota(jnp.int32, (T, T), 0)
    si = lax.broadcasted_iota(jnp.int32, (T, T), 1)
    ld = ld_ref[...]
    cum[...] = dot((ti >= si).astype(F32), ld, ((1,), (1,)), precision=lax.Precision.HIGHEST)
    tail_w[...] = jnp.exp(cum[T - 1 : T, :] - cum[...])
    head_w[...] = jnp.exp(cum[...])
    cum_t[...] = dot(ld, (ti <= si).astype(F32), precision=lax.Precision.HIGHEST)
    lane_head = lax.broadcasted_iota(jnp.int32, (T, heads), 1)

    def cols(h):
        return pl.ds(pl.multiple_of(h * hd, hd), hd)

    def column(ref, h):
        return jnp.sum(jnp.where(lane_head == h, ref[...], 0.0), axis=1, keepdims=True)

    dec[...] = jnp.broadcast_to(jnp.exp(cum_t[:, T - 1 : T]), dec.shape)

    @pl.when(plane == 0)
    def _():
        cin[...] = jnp.zeros_like(cin)

    def state(h):
        wk = (column(tail_w, h) * k[:, cols(h)].astype(F32)).astype(BF16)
        return dot(wk, v[:, cols(h)], ((0,), (0,)))

    d_copy = remote(dec, pdec, d_send, d_recv, partner)
    e_copy = remote(cdec, odec, e_send, e_recv, across)

    def a_copy(a):
        part = st.at[0], rst.at[0]
        if a:
            some = pl.ds((a - 1) * (hq // 2), hq // 2)
            part = st.at[1, some], rst.at[1, some]
        return remote(*part, a_send.at[a], a_recv.at[a], partner)

    def x_copy(i):
        return remote(sx.at[i], rx.at[i], x_send.at[i], x_recv.at[i], across)

    def b_copy(i):
        return remote(cout.at[i], cin.at[i], b_send.at[i], b_recv.at[i], jnp.minimum(me + PLANE, n - 1))

    def y_copy(i):
        return remote(xs.at[i], xr.at[i], y_send.at[i], y_recv.at[i], across)

    def c_copy(a, i):
        return remote(cs.at[a, i], cr.at[a, i], c_send.at[a, i], c_recv.at[a, i], partner)

    def row(ref, h):
        return ref[pl.ds(h, 1), :]

    def states(to, a, far_core, lo, hi):
        def step(i, z):
            to[a, i] = state(head_of(a, far_core, i))
            return z
        lax.fori_loop(lo, hi, step, 0, unroll=hi - lo)

    def both(a, i):
        h = head_of(a, 0, i)
        mine, theirs = own[a, i], rst[a, i]
        early, late = jnp.where(first_core, mine, theirs), jnp.where(first_core, theirs, mine)
        return jnp.where(first_core, row(pdec, h), row(dec, h)) * early + late

    def across_step(i, z):
        sx[i] = both(1, i).astype(BF16)
        x_copy(i).start()
        return z

    hh = hq // 2
    experts = n
    ids = ids_ref[...]
    ex = lax.broadcasted_iota(jnp.int32, (experts, T), 0)
    first, second = (ids[0:1, :] == ex).astype(F32), (ids[1:2, :] == ex).astype(F32)
    earlier = dot((first + second).astype(BF16), (ti < si).astype(BF16))
    place = earlier + (ex * capp).astype(F32)
    row_of = [jnp.sum(one * place, axis=0, keepdims=True) for one in (first, second)]
    goal[0:1, :] = row_of[0]
    goal[1:2, :] = row_of[1]
    goal[2:8, :] = jnp.full((6, T), -1.0, F32)
    goal_copy = pltpu.make_async_remote_copy(
        goal, goal_in.at[land_slot], g_send, g_recv.at[land_slot],
        device_id={"ctx": lander}, device_id_type=pl.DeviceIdType.MESH)
    slot = lax.broadcasted_iota(jnp.int32, (half_n * capp, T), 0) + base * capp
    slot = slot.astype(F32)
    disp[0] = ((slot == row_of[0]) | (slot == row_of[1])).astype(BF16)

    wait_quarter(0)
    start_quarter(2)
    states(st, 1, 1, 0, hh)
    pl.semaphore_wait(barrier, 2 + beside)
    tell_column(column_in.at[0])
    d_copy.start()
    a_copy(1).start()
    states(st, 1, 1, hh, hq)
    a_copy(2).start()
    wait_quarter(1)
    start_quarter(3)
    q_load.start()
    states(own, 1, 0, 0, hh)
    d_copy.wait_recv()
    cdec[...] = dec[...] * pdec[...]
    e_copy.start()
    states(own, 1, 0, hh, hq)
    a_copy(1).wait_recv()
    lax.fori_loop(0, hh, across_step, 0)
    wait_quarter(2)
    gate_load.start()
    states(st, 0, 1, 0, hh)
    a_copy(2).wait_recv()
    lax.fori_loop(hh, hq, across_step, 0)
    states(st, 0, 1, hh, hq)
    a_copy(0).start()
    wait_quarter(3)
    res_load.start()
    states(own, 0, 0, 0, hh)
    states(own, 0, 0, hh, hq)
    a_copy(0).wait_recv()
    e_copy.wait_recv()

    def give(a, i, x):
        h = head_of(a, 0, i)
        after = (jnp.where(first_core, row(dec, h), row(pdec, h)) * x
                 + jnp.where(first_core, own[a, i], rst[a, i])).astype(BF16)
        x = x.astype(BF16)
        co[a, i] = jnp.where(first_core, x, after)
        cs[a, i] = jnp.where(first_core, after, x)
        c_copy(a, i).start()

    def scan_step(i):
        @pl.when(plane > 0)
        def _():
            b_copy(i).wait_recv()

        x_copy(i).wait_recv()
        h = head_of(0, 0, i)
        mine, theirs = both(0, i), rx[i].astype(F32)
        d_mine, d_theirs = row(cdec, h), row(odec, h)
        x = cin[i].astype(F32)
        mid = jnp.where(first_chip, d_mine, d_theirs) * x + jnp.where(first_chip, mine, theirs)
        last = jnp.where(first_chip, d_theirs, d_mine) * mid + jnp.where(first_chip, theirs, mine)
        cout[i] = last.astype(BF16)

        @pl.when(plane < planes - 1)
        def _():
            b_copy(i).start()

        xs[i] = jnp.where(first_chip, mid, x).astype(BF16)
        y_copy(i).start()
        give(0, i, jnp.where(first_chip, x, mid))

    def far_step(i):
        y_copy(i).wait_recv()
        give(1, i, xr[i].astype(F32))

    q_load.wait()
    mask = ti >= si

    def intra_step(i):
        hs = [head_of(a, b, i) for a in range(2) for b in range(2)]
        scores = [dot(q[:, cols(h)], k[:, cols(h)], ((1,), (1,))) for h in hs]
        weights = [
            jnp.where(mask, x * jnp.exp(column(cum, h) - row(cum_t, h)), 0.0).astype(BF16)
            for x, h in zip(scores, hs)
        ]
        for w, h in zip(weights, hs):
            att[:, cols(h)] = dot(w, v[:, cols(h)])

    def gate_step(i):
        for j in range(PLANE):
            h = i * PLANE + j
            gated[:, cols(h)] = jax.nn.sigmoid(gate[:, cols(h)].astype(F32)) * again_ref[:, cols(h)]

    def inter_step(i):
        for a in range(2):
            c_copy(a, i).wait_recv()
        total = ss[...]
        for a in range(2):
            for b, carried in enumerate((co, cr)):
                h = head_of(a, b, i)
                x = att[:, cols(h)] + column(head_w, h) * dot(q[:, cols(h)], carried[a, i])
                att[:, cols(h)] = x
                total += x * x
        ss[...] = total

    ss[...] = jnp.zeros_like(ss)
    gate_load.wait()
    scan_at = START + HOP * plane
    far_at = jnp.maximum(scan_at + LAG, FAR)
    inter_at = far_at + LAG

    def during(i, at, step):
        @pl.when((i >= at) & (i < at + hq))
        def _():
            step(i - at)

    def meet(i):
        for r in range(planes):
            @pl.when(i == (r + 1) * GAP)
            def _():
                if r < planes - 2:
                    pl.semaphore_wait(column_in.at[r], beside)
                if r < planes - 3:
                    tell_column(column_in.at[r + 1])
                if r == planes - 3:
                    tell(across_in, across)
                if r == planes - 2:
                    pl.semaphore_wait(across_in, 1)
                    tell(partner_in, partner)
                if r == planes - 1:
                    pl.semaphore_wait(partner_in, 1)
                    goal_copy.start()

    def mixed_step(i, z):
        meet(i)
        during(i, scan_at, scan_step)
        during(i, far_at, far_step)
        during(i, 0, intra_step)
        during(i, hq, gate_step)
        during(i, inter_at, inter_step)
        return z

    lax.fori_loop(0, jnp.maximum(hq, inter_at) + hq, mixed_step, 0)

    rstd = lax.rsqrt(jnp.sum(ss[...], axis=1, keepdims=True) / D + 1e-6)
    res_load.wait()
    ss[...] = jnp.zeros_like(ss)

    def branch_step(i, z):
        total = ss[...]
        for j in range(BRANCH):
            h = i * BRANCH + j
            x = att[:, cols(h)] * rstd * gated[:, cols(h)]
            x = res[:, cols(h)].astype(F32) + x
            att[:, cols(h)] = x
            total += x * x
        ss[...] = total
        return z

    lax.fori_loop(0, heads // BRANCH, branch_step, 0)
    rstd2 = lax.rsqrt(jnp.sum(ss[...], axis=1, keepdims=True) / D + 1e-6)
    wide = D // PARTS

    def part(c):
        return pl.ds(pl.multiple_of(c * wide, wide), wide)

    def each_piece(step):
        lax.fori_loop(0, PARTS - 1, lambda c, z: (step(c, part(c)), z)[1], 0)
        for t in range(2):
            step(PARTS - 1 + t, pl.ds(D - wide + t * (wide // 2), wide // 2))

    def l_copy(c, at, x):
        return remote(normed.at[:, at], landed.at[x, :, at], l_send.at[c], l_recv.at[x, c], lander)

    def norm_step(c, at):
        normed[:, at] = (att[:, at] * rstd2 * mgain_ref[:, at]).astype(BF16)
        l_copy(c, at, land_slot).start()

    each_piece(norm_step)

    def near_step(c, _):
        rows = dot(disp[0], normed[:, part(c)]).astype(BF16)
        for e in range(half_n):
            near[e, :, part(c)] = rows[e * capp : e * capp + cap]
        return 0

    lax.fori_loop(0, PARTS, near_step, 0)

    def n_copy(j):
        e = (local + j) % half_n
        return pltpu.make_async_remote_copy(
            near.at[e], out_ref.at[me], n_send.at[j], n_recv.at[j],
            device_id={"ctx": base + e}, device_id_type=pl.DeviceIdType.MESH)

    keep = pltpu.make_async_copy(near.at[local], out_ref.at[me], n_send.at[0])
    keep.start()
    for j in range(1, half_n):
        n_copy(j).start()

    @pl.when(lands)
    def _():
        for x in range(2):
            pltpu.make_async_remote_copy(
                goal, goal_in.at[x], g_send, g_recv.at[x],
                device_id={"ctx": lander}, device_id_type=pl.DeviceIdType.MESH).wait_recv()
            disp[1 + x] = ((slot == goal_in[x, 0:1, :]) | (slot == goal_in[x, 1:2, :])).astype(BF16)

        def relayed(c, at):
            return remote(relay.at[:, :, at], relay.at[:, :, at], r_send.at[c], r_recv.at[0], lander)

        def relay_from(x, again):
            block = (far + x) * PLANE + rank

            def step(c, at):
                if again:
                    relayed(c, at).wait_send()
                l_copy(c, at, x).wait_recv()
                rows = dot(disp[1 + x], landed[x, :, at]).astype(BF16)
                for e in range(half_n):
                    relay[e, :, at] = rows[e * capp : e * capp + cap]
                for j in range(1, half_n):
                    e = (local + j) % half_n
                    remote(relay.at[e, :, at], out_ref.at[block, :, at],
                           r_send.at[c], r_recv.at[block - (half_n - base)], base + e).start()
                pltpu.make_async_copy(relay.at[local, :, at], out_ref.at[block, :, at], r_send.at[c]).start()

            each_piece(step)

        relay_from(1 - upper, False)
        relay_from(upper, True)
        each_piece(lambda c, at: relayed(c, at).wait_send())

    keep.wait()
    for j in range(1, half_n):
        n_copy(j).wait()
    first = far * PLANE + rank - (half_n - base)
    for b in range(half_n):
        @pl.when(jnp.logical_not(lands & ((b == first) | (b == first + PLANE))))
        def _():
            pltpu.make_async_copy(near.at[0], out_ref.at[half_n - base + b], r_recv.at[b]).wait()
    each_piece(lambda c, at: l_copy(c, at, land_slot).wait_send())
    goal_copy.wait_send()
    d_copy.wait_send()
    e_copy.wait_send()
    for a in range(3):
        a_copy(a).wait_send()

    def sent(i, z):
        x_copy(i).wait_send()
        y_copy(i).wait_send()
        for a in range(2):
            c_copy(a, i).wait_send()
        return z

    lax.fori_loop(0, hq, sent, 0)

    @pl.when(plane < planes - 1)
    def _():
        lax.fori_loop(0, hq, lambda i, z: (b_copy(i).wait_send(), z)[1], 0)


def body(query, key_rows, value_rows, log_decay, gate_input, residual, attn_gain, moe_gain, expert_ids):
    T, D = query.shape
    heads = log_decay.shape[1]
    hd = D // heads
    n = lax.axis_size("ctx")
    experts = n
    cap = 5 * T * expert_ids.shape[1] // (4 * experts)
    hq = heads // PLANE
    capp = -(-cap // 16) * 16
    half_n = n // 2
    vm, anyspace = pl.BlockSpec(memory_space=pltpu.VMEM), pl.BlockSpec(memory_space=pl.ANY)
    V, DMA, REG = pltpu.VMEM, pltpu.SemaphoreType.DMA, pltpu.SemaphoreType.REGULAR
    arrived = pl.pallas_call(
        functools.partial(attend_kernel, (n, heads, hd, cap, capp)),
        out_shape=pltpu.VMEM((n, cap, D), BF16),
        in_specs=[anyspace] * 3 + [vm] + [anyspace] * 2 + [vm] * 3,
        out_specs=anyspace,
        scratch_shapes=[
            V((T, D), BF16), V((T, D), BF16), V((T, D), BF16), V((T, D), BF16), V((T, D), BF16),
            V((T, D), F32), V((T, heads), F32), V((T, heads), F32), V((T, heads), F32), V((heads, T), F32), V((T, hd), F32),
            V((3, half_n * capp, T), BF16),
            V((heads, 128), F32), V((heads, 128), F32), V((heads, 128), F32), V((heads, 128), F32),
            V((2, hq, hd, hd), F32), V((2, hq, hd, hd), F32), V((2, hq, hd, hd), F32),
            V((hq, hd, hd), BF16), V((hq, hd, hd), BF16), V((hq, hd, hd), BF16), V((hq, hd, hd), BF16),
            V((hq, hd, hd), BF16), V((hq, hd, hd), BF16),
            V((2, hq, hd, hd), BF16), V((2, hq, hd, hd), BF16), V((2, hq, hd, hd), BF16),
            V((8, T), F32), V((2, 8, T), F32), V((T, D), F32), V((2, T, D), BF16),
            V((half_n, cap, D), BF16), V((half_n, cap, D), BF16),
            DMA((11,)), DMA, DMA, DMA, DMA, DMA((3,)), DMA((3,)), DMA((hq,)), DMA((hq,)), DMA((hq,)), DMA((hq,)),
            DMA((hq,)), DMA((hq,)), DMA((2, hq)), DMA((2, hq)),
            DMA, DMA((2,)), DMA((PARTS + 1,)), DMA((2, PARTS + 1)), DMA((half_n,)), DMA((half_n,)),
            DMA((PARTS + 1,)), DMA((half_n,)), REG((n // PLANE - 2,)), REG, REG,
        ],
        compiler_params=pltpu.CompilerParams(
            collective_id=0, has_side_effects=True, vmem_limit_bytes=57000000
        ),
        name="attend",
    )(
        query, key_rows, value_rows, log_decay.T, gate_input, residual,
        attn_gain.reshape(1, D), moe_gain.reshape(1, D), expert_ids.T,
    )
    return arrived.reshape(1, n * cap, D)


def solution(mesh):
    rows = P(("groups", "ctx"), None)
    return jax.shard_map(
        body, mesh=mesh, in_specs=(rows,) * 6 + (P(), P(), rows),
        out_specs=P(("groups", "ctx"), None, None), check_vma=False,
    )
```

```python
import functools

import jax
import jax.numpy as jnp
from jax import lax
from jax.experimental import pallas as pl
from jax.experimental.pallas import tpu as pltpu
from jax.sharding import PartitionSpec as P

PLANE = 4
START = 0
HOP = 3
LAG = 3
FAR = 11
GAP = 2
BRANCH = 4
PARTS = 24
F32 = jnp.float32
BF16 = jnp.bfloat16


def dot(a, b, dims=((1,), (0,)), precision=None):
    return lax.dot_general(a, b, (dims, ((), ())), preferred_element_type=F32, precision=precision)


def attend_kernel(
    sizes, q_hbm, k_hbm, v_hbm, ld_ref, gate_hbm, res_hbm, again_ref, mgain_ref, ids_ref, out_ref,
    q, k, v, gate, res, att, cum, tail_w, head_w, cum_t, ss, disp,
    dec, pdec, cdec, odec, own, st, rst, sx, rx, cin, cout, xs, xr, co, cs, cr,
    goal, goal_in, gated, landed, near, relay,
    in_sem, d_send, d_recv, e_send, e_recv, a_send, a_recv, x_send, x_recv, b_send, b_recv,
    y_send, y_recv, c_send, c_recv,
    g_send, g_recv, l_send, l_recv, n_send, n_recv, r_send, r_recv, column_in, across_in, partner_in,
):
    n, heads, hd, cap, capp = sizes
    normed = k
    T, D = att.shape
    hq = heads // PLANE
    planes = n // PLANE
    me = lax.axis_index("ctx")
    plane, rank = me // PLANE, me % PLANE
    half_n = n // 2
    half_p = planes // 2
    upper = (plane >= half_p).astype(jnp.int32)
    base = upper * half_n
    local = me - base
    inner = jnp.where(upper == 1, plane - half_p, half_p - 1 - plane)
    outer = jnp.where(upper == 1, plane - half_p, plane)
    lander = jnp.where(upper == 1, half_p - 1 - outer // 2, half_p + outer // 2) * PLANE + rank
    land_slot = outer % 2
    lands = inner < half_p // 2
    far = jnp.minimum(2 * inner, half_p - 2) + (1 - upper) * half_p

    core, chip = rank % 2, rank // 2
    first_core, first_chip = core == 0, chip == 0
    partner = me + 1 - 2 * core
    across = me + 2 - 4 * chip

    def remote(src, dst, send, recv, to):
        return pltpu.make_async_remote_copy(
            src, dst, send, recv, device_id={"ctx": to}, device_id_type=pl.DeviceIdType.MESH)

    def head_of(far_chip, far_core, i):
        c = 1 - chip if far_chip else chip
        return (2 * c + (1 - core if far_core else core)) * hq + i

    quarters = [(1, 1), (1, 0), (0, 1), (0, 0)]

    def quarter_load(i):
        at = pl.ds(pl.multiple_of(head_of(*quarters[i], 0) * hd, hd), hq * hd)
        return [
            pltpu.make_async_copy(src.at[:, at], dst.at[:, at], in_sem.at[2 * i + j])
            for j, (src, dst) in enumerate(((k_hbm, k), (v_hbm, v)))
        ]

    def start_quarter(i):
        for load in quarter_load(i):
            load.start()

    def wait_quarter(i):
        for load in quarter_load(i):
            load.wait()

    q_load, gate_load, res_load = (
        pltpu.make_async_copy(src, dst, in_sem.at[8 + i])
        for i, (src, dst) in enumerate(((q_hbm, q), (gate_hbm, gate), (res_hbm, res)))
    )
    start_quarter(0)
    start_quarter(1)

    barrier = pltpu.get_barrier_semaphore()

    def tell(sem, to):
        pl.semaphore_signal(sem, inc=1, device_id={"ctx": to}, device_id_type=pl.DeviceIdType.MESH)

    def tell_column(sem):
        @pl.when(plane > 0)
        def _():
            tell(sem, me - PLANE)

        @pl.when(plane < planes - 1)
        def _():
            tell(sem, me + PLANE)

    beside = (plane > 0).astype(jnp.int32) + (plane < planes - 1).astype(jnp.int32)
    tell(barrier, partner)
    tell(barrier, across)
    tell_column(barrier)

    ti = lax.broadcasted_iota(jnp.int32, (T, T), 0)
    si = lax.broadcasted_iota(jnp.int32, (T, T), 1)
    ld = ld_ref[...]
    cum[...] = dot((ti >= si).astype(F32), ld, ((1,), (1,)), precision=lax.Precision.HIGHEST)
    tail_w[...] = jnp.exp(cum[T - 1 : T, :] - cum[...])
    head_w[...] = jnp.exp(cum[...])
    cum_t[...] = dot(ld, (ti <= si).astype(F32), precision=lax.Precision.HIGHEST)
    lane_head = lax.broadcasted_iota(jnp.int32, (T, heads), 1)

    def cols(h):
        return pl.ds(pl.multiple_of(h * hd, hd), hd)

    def column(ref, h):
        return jnp.sum(jnp.where(lane_head == h, ref[...], 0.0), axis=1, keepdims=True)

    dec[...] = jnp.broadcast_to(jnp.exp(cum_t[:, T - 1 : T]), dec.shape)

    @pl.when(plane == 0)
    def _():
        cin[...] = jnp.zeros_like(cin)

    def state(h):
        wk = (column(tail_w, h) * k[:, cols(h)].astype(F32)).astype(BF16)
        return dot(wk, v[:, cols(h)], ((0,), (0,)))

    d_copy = remote(dec, pdec, d_send, d_recv, partner)
    e_copy = remote(cdec, odec, e_send, e_recv, across)

    def a_copy(a):
        part = st.at[0], rst.at[0]
        if a:
            some = pl.ds((a - 1) * (hq // 2), hq // 2)
            part = st.at[1, some], rst.at[1, some]
        return remote(*part, a_send.at[a], a_recv.at[a], partner)

    def x_copy(i):
        return remote(sx.at[i], rx.at[i], x_send.at[i], x_recv.at[i], across)

    def b_copy(i):
        return remote(cout.at[i], cin.at[i], b_send.at[i], b_recv.at[i], jnp.minimum(me + PLANE, n - 1))

    def y_copy(i):
        return remote(xs.at[i], xr.at[i], y_send.at[i], y_recv.at[i], across)

    def c_copy(a, i):
        return remote(cs.at[a, i], cr.at[a, i], c_send.at[a, i], c_recv.at[a, i], partner)

    def row(ref, h):
        return ref[pl.ds(h, 1), :]

    def states(to, a, far_core, lo, hi):
        def step(i, z):
            to[a, i] = state(head_of(a, far_core, i))
            return z
        lax.fori_loop(lo, hi, step, 0, unroll=hi - lo)

    def both(a, i):
        h = head_of(a, 0, i)
        mine, theirs = own[a, i], rst[a, i]
        early, late = jnp.where(first_core, mine, theirs), jnp.where(first_core, theirs, mine)
        return jnp.where(first_core, row(pdec, h), row(dec, h)) * early + late

    def across_step(i, z):
        sx[i] = both(1, i).astype(BF16)
        x_copy(i).start()
        return z

    hh = hq // 2
    experts = n
    ids = ids_ref[...]
    ex = lax.broadcasted_iota(jnp.int32, (experts, T), 0)
    first, second = (ids[0:1, :] == ex).astype(F32), (ids[1:2, :] == ex).astype(F32)
    earlier = dot((first + second).astype(BF16), (ti < si).astype(BF16))
    place = earlier + (ex * capp).astype(F32)
    row_of = [jnp.sum(one * place, axis=0, keepdims=True) for one in (first, second)]
    goal[0:1, :] = row_of[0]
    goal[1:2, :] = row_of[1]
    goal[2:8, :] = jnp.full((6, T), -1.0, F32)
    goal_copy = pltpu.make_async_remote_copy(
        goal, goal_in.at[land_slot], g_send, g_recv.at[land_slot],
        device_id={"ctx": lander}, device_id_type=pl.DeviceIdType.MESH)
    slot = lax.broadcasted_iota(jnp.int32, (half_n * capp, T), 0) + base * capp
    slot = slot.astype(F32)
    disp[0] = ((slot == row_of[0]) | (slot == row_of[1])).astype(BF16)

    wait_quarter(0)
    start_quarter(2)
    states(st, 1, 1, 0, hh)
    pl.semaphore_wait(barrier, 2 + beside)
    tell_column(column_in.at[0])
    d_copy.start()
    a_copy(1).start()
    states(st, 1, 1, hh, hq)
    a_copy(2).start()
    wait_quarter(1)
    start_quarter(3)
    q_load.start()
    states(own, 1, 0, 0, hh)
    d_copy.wait_recv()
    cdec[...] = dec[...] * pdec[...]
    e_copy.start()
    states(own, 1, 0, hh, hq)
    a_copy(1).wait_recv()
    lax.fori_loop(0, hh, across_step, 0)
    wait_quarter(2)
    gate_load.start()
    states(st, 0, 1, 0, hh)
    a_copy(2).wait_recv()
    lax.fori_loop(hh, hq, across_step, 0)
    states(st, 0, 1, hh, hq)
    a_copy(0).start()
    wait_quarter(3)
    res_load.start()
    states(own, 0, 0, 0, hh)
    states(own, 0, 0, hh, hq)
    a_copy(0).wait_recv()
    e_copy.wait_recv()

    def give(a, i, x):
        h = head_of(a, 0, i)
        after = (jnp.where(first_core, row(dec, h), row(pdec, h)) * x
                 + jnp.where(first_core, own[a, i], rst[a, i])).astype(BF16)
        x = x.astype(BF16)
        co[a, i] = jnp.where(first_core, x, after)
        cs[a, i] = jnp.where(first_core, after, x)
        c_copy(a, i).start()

    def scan_step(i):
        @pl.when(plane > 0)
        def _():
            b_copy(i).wait_recv()

        x_copy(i).wait_recv()
        h = head_of(0, 0, i)
        mine, theirs = both(0, i), rx[i].astype(F32)
        d_mine, d_theirs = row(cdec, h), row(odec, h)
        x = cin[i].astype(F32)
        mid = jnp.where(first_chip, d_mine, d_theirs) * x + jnp.where(first_chip, mine, theirs)
        last = jnp.where(first_chip, d_theirs, d_mine) * mid + jnp.where(first_chip, theirs, mine)
        cout[i] = last.astype(BF16)

        @pl.when(plane < planes - 1)
        def _():
            b_copy(i).start()

        xs[i] = jnp.where(first_chip, mid, x).astype(BF16)
        y_copy(i).start()
        give(0, i, jnp.where(first_chip, x, mid))

    def far_step(i):
        y_copy(i).wait_recv()
        give(1, i, xr[i].astype(F32))

    q_load.wait()
    mask = ti >= si

    def intra_step(i):
        hs = [head_of(a, b, i) for a in range(2) for b in range(2)]
        scores = [dot(q[:, cols(h)], k[:, cols(h)], ((1,), (1,))) for h in hs]
        weights = [
            jnp.where(mask, x * jnp.exp(column(cum, h) - row(cum_t, h)), 0.0).astype(BF16)
            for x, h in zip(scores, hs)
        ]
        for w, h in zip(weights, hs):
            att[:, cols(h)] = dot(w, v[:, cols(h)])

    def gate_step(i):
        for j in range(PLANE):
            h = i * PLANE + j
            gated[:, cols(h)] = jax.nn.sigmoid(gate[:, cols(h)].astype(F32)) * again_ref[:, cols(h)]

    def inter_step(i):
        for a in range(2):
            c_copy(a, i).wait_recv()
        total = ss[...]
        for a in range(2):
            for b, carried in enumerate((co, cr)):
                h = head_of(a, b, i)
                x = att[:, cols(h)] + column(head_w, h) * dot(q[:, cols(h)], carried[a, i])
                att[:, cols(h)] = x
                total += x * x
        ss[...] = total

    ss[...] = jnp.zeros_like(ss)
    gate_load.wait()
    scan_at = START + HOP * plane
    far_at = jnp.maximum(scan_at + LAG, FAR)
    inter_at = far_at + LAG - 1

    def during(i, at, step):
        @pl.when((i >= at) & (i < at + hq))
        def _():
            step(i - at)

    def meet(i):
        for r in range(planes):
            @pl.when(i == (r + 1) * GAP)
            def _():
                if r < planes - 2:
                    pl.semaphore_wait(column_in.at[r], beside)
                if r < planes - 3:
                    tell_column(column_in.at[r + 1])
                if r == planes - 3:
                    tell(across_in, across)
                if r == planes - 2:
                    pl.semaphore_wait(across_in, 1)
                    tell(partner_in, partner)
                if r == planes - 1:
                    pl.semaphore_wait(partner_in, 1)
                    goal_copy.start()

    def mixed_step(i, z):
        meet(i)
        during(i, scan_at, scan_step)
        during(i, far_at, far_step)
        during(i, 0, intra_step)
        during(i, hq, gate_step)
        during(i, inter_at, inter_step)
        return z

    lax.fori_loop(0, jnp.maximum(hq, inter_at) + hq, mixed_step, 0)

    rstd = lax.rsqrt(jnp.sum(ss[...], axis=1, keepdims=True) / D + 1e-6)
    res_load.wait()
    ss[...] = jnp.zeros_like(ss)

    def branch_step(i, z):
        total = ss[...]
        for j in range(BRANCH):
            h = i * BRANCH + j
            x = att[:, cols(h)] * rstd * gated[:, cols(h)]
            x = res[:, cols(h)].astype(F32) + x
            att[:, cols(h)] = x
            total += x * x
        ss[...] = total
        return z

    lax.fori_loop(0, heads // BRANCH, branch_step, 0)
    rstd2 = lax.rsqrt(jnp.sum(ss[...], axis=1, keepdims=True) / D + 1e-6)
    wide = D // PARTS

    def part(c):
        return pl.ds(pl.multiple_of(c * wide, wide), wide)

    def each_piece(step):
        lax.fori_loop(0, PARTS - 1, lambda c, z: (step(c, part(c)), z)[1], 0)
        for t in range(2):
            step(PARTS - 1 + t, pl.ds(D - wide + t * (wide // 2), wide // 2))

    def l_copy(c, at, x):
        return remote(normed.at[:, at], landed.at[x, :, at], l_send.at[c], l_recv.at[x, c], lander)

    def norm_step(c, at):
        normed[:, at] = (att[:, at] * rstd2 * mgain_ref[:, at]).astype(BF16)
        l_copy(c, at, land_slot).start()

    each_piece(norm_step)

    def near_step(c, _):
        rows = dot(disp[0], normed[:, part(c)]).astype(BF16)
        for e in range(half_n):
            near[e, :, part(c)] = rows[e * capp : e * capp + cap]
        return 0

    lax.fori_loop(0, PARTS, near_step, 0)

    def n_copy(j):
        e = (local + j) % half_n
        return pltpu.make_async_remote_copy(
            near.at[e], out_ref.at[me], n_send.at[j], n_recv.at[j],
            device_id={"ctx": base + e}, device_id_type=pl.DeviceIdType.MESH)

    keep = pltpu.make_async_copy(near.at[local], out_ref.at[me], n_send.at[0])
    keep.start()
    for j in range(1, half_n):
        n_copy(j).start()

    @pl.when(lands)
    def _():
        for x in range(2):
            pltpu.make_async_remote_copy(
                goal, goal_in.at[x], g_send, g_recv.at[x],
                device_id={"ctx": lander}, device_id_type=pl.DeviceIdType.MESH).wait_recv()
            disp[1 + x] = ((slot == goal_in[x, 0:1, :]) | (slot == goal_in[x, 1:2, :])).astype(BF16)

        def relayed(c, at):
            return remote(relay.at[:, :, at], relay.at[:, :, at], r_send.at[c], r_recv.at[0], lander)

        def relay_from(x, again):
            block = (far + x) * PLANE + rank

            def step(c, at):
                if again:
                    relayed(c, at).wait_send()
                l_copy(c, at, x).wait_recv()
                rows = dot(disp[1 + x], landed[x, :, at]).astype(BF16)
                for e in range(half_n):
                    relay[e, :, at] = rows[e * capp : e * capp + cap]
                for j in range(1, half_n):
                    e = (local + j) % half_n
                    remote(relay.at[e, :, at], out_ref.at[block, :, at],
                           r_send.at[c], r_recv.at[block - (half_n - base)], base + e).start()
                pltpu.make_async_copy(relay.at[local, :, at], out_ref.at[block, :, at], r_send.at[c]).start()

            each_piece(step)

        relay_from(1 - upper, False)
        relay_from(upper, True)
        each_piece(lambda c, at: relayed(c, at).wait_send())

    keep.wait()
    for j in range(1, half_n):
        n_copy(j).wait()
    first = far * PLANE + rank - (half_n - base)
    for b in range(half_n):
        @pl.when(jnp.logical_not(lands & ((b == first) | (b == first + PLANE))))
        def _():
            pltpu.make_async_copy(near.at[0], out_ref.at[half_n - base + b], r_recv.at[b]).wait()
    each_piece(lambda c, at: l_copy(c, at, land_slot).wait_send())
    goal_copy.wait_send()
    d_copy.wait_send()
    e_copy.wait_send()
    for a in range(3):
        a_copy(a).wait_send()

    def sent(i, z):
        x_copy(i).wait_send()
        y_copy(i).wait_send()
        for a in range(2):
            c_copy(a, i).wait_send()
        return z

    lax.fori_loop(0, hq, sent, 0)

    @pl.when(plane < planes - 1)
    def _():
        lax.fori_loop(0, hq, lambda i, z: (b_copy(i).wait_send(), z)[1], 0)


def body(query, key_rows, value_rows, log_decay, gate_input, residual, attn_gain, moe_gain, expert_ids):
    T, D = query.shape
    heads = log_decay.shape[1]
    hd = D // heads
    n = lax.axis_size("ctx")
    experts = n
    cap = 5 * T * expert_ids.shape[1] // (4 * experts)
    hq = heads // PLANE
    capp = -(-cap // 16) * 16
    half_n = n // 2
    vm, anyspace = pl.BlockSpec(memory_space=pltpu.VMEM), pl.BlockSpec(memory_space=pl.ANY)
    V, DMA, REG = pltpu.VMEM, pltpu.SemaphoreType.DMA, pltpu.SemaphoreType.REGULAR
    arrived = pl.pallas_call(
        functools.partial(attend_kernel, (n, heads, hd, cap, capp)),
        out_shape=pltpu.VMEM((n, cap, D), BF16),
        in_specs=[anyspace] * 3 + [vm] + [anyspace] * 2 + [vm] * 3,
        out_specs=anyspace,
        scratch_shapes=[
            V((T, D), BF16), V((T, D), BF16), V((T, D), BF16), V((T, D), BF16), V((T, D), BF16),
            V((T, D), F32), V((T, heads), F32), V((T, heads), F32), V((T, heads), F32), V((heads, T), F32), V((T, hd), F32),
            V((3, half_n * capp, T), BF16),
            V((heads, 128), F32), V((heads, 128), F32), V((heads, 128), F32), V((heads, 128), F32),
            V((2, hq, hd, hd), F32), V((2, hq, hd, hd), F32), V((2, hq, hd, hd), F32),
            V((hq, hd, hd), BF16), V((hq, hd, hd), BF16), V((hq, hd, hd), BF16), V((hq, hd, hd), BF16),
            V((hq, hd, hd), BF16), V((hq, hd, hd), BF16),
            V((2, hq, hd, hd), BF16), V((2, hq, hd, hd), BF16), V((2, hq, hd, hd), BF16),
            V((8, T), F32), V((2, 8, T), F32), V((T, D), F32), V((2, T, D), BF16),
            V((half_n, cap, D), BF16), V((half_n, cap, D), BF16),
            DMA((11,)), DMA, DMA, DMA, DMA, DMA((3,)), DMA((3,)), DMA((hq,)), DMA((hq,)), DMA((hq,)), DMA((hq,)),
            DMA((hq,)), DMA((hq,)), DMA((2, hq)), DMA((2, hq)),
            DMA, DMA((2,)), DMA((PARTS + 1,)), DMA((2, PARTS + 1)), DMA((half_n,)), DMA((half_n,)),
            DMA((PARTS + 1,)), DMA((half_n,)), REG((n // PLANE - 2,)), REG, REG,
        ],
        compiler_params=pltpu.CompilerParams(
            collective_id=0, has_side_effects=True, vmem_limit_bytes=57000000
        ),
        name="attend",
    )(
        query, key_rows, value_rows, log_decay.T, gate_input, residual,
        attn_gain.reshape(1, D), moe_gain.reshape(1, D), expert_ids.T,
    )
    return arrived.reshape(1, n * cap, D)


def solution(mesh):
    rows = P(("groups", "ctx"), None)
    return jax.shard_map(
        body, mesh=mesh, in_specs=(rows,) * 6 + (P(), P(), rows),
        out_specs=P(("groups", "ctx"), None, None), check_vma=False,
    )
```
